32 devices in a mesh: ctx: 8 (over z, x), fsdp: 4 (over y, core).
Axes of the slice: x: 2, y: 2, z: 4, core: 2. Of those that a mesh axis runs over, the one named last changes fastest.
Arguments:
- inputs: bfloat16 [4, 1024, 768], P('fsdp', 'ctx'), may hold values from -6 to 6
- block_order: int32 [16], replicated, may hold values from 0 to 15, each once
- cotangent: bfloat16 [4, 1024, 768], P('fsdp', 'ctx'), may hold values from -6 to 6
- first_gain: bfloat16 [768], P('fsdp'), may hold values from 0.25 to 1.75
- first_shift: bfloat16 [768], P('fsdp'), may hold values from -3 to 3
- qkv_weight: bfloat16 [768, 2304], P('fsdp')
- qv_bias: bfloat16 [1536], P('fsdp'), may hold values from -3 to 3
- proj_weight: bfloat16 [768, 768], P('fsdp'), may hold values from -1.75 to 1.75
- proj_bias: bfloat16 [768], P('fsdp'), may hold values from -3 to 3
- second_gain: bfloat16 [768], P('fsdp'), may hold values from 0.25 to 1.75
- second_shift: bfloat16 [768], P('fsdp'), may hold values from -3 to 3
- fc_weight: bfloat16 [768, 3072], P('fsdp'), may hold values from -0.21875 to 0.21875
- fc_bias: bfloat16 [3072], P('fsdp'), may hold values from -3 to 3
- down_weight: bfloat16 [3072, 768], P('fsdp'), may hold values from -0.109375 to 0.109375
- down_bias: bfloat16 [768], P('fsdp'), may hold values from -3 to 3
Outputs:
- block_out: bfloat16 [4, 1024, 768], P('fsdp', 'ctx')
- grad_input: float32 [4, 1024, 768], P('fsdp', 'ctx')
- grad_first_gain: float32 [768], P(('ctx', 'fsdp'))
- grad_first_shift: float32 [768], P(('ctx', 'fsdp'))
- grad_qkv_weight: float32 [768, 2304], P('fsdp', 'ctx')
- grad_qv_bias: float32 [1536], P(('ctx', 'fsdp'))
- grad_proj_weight: float32 [768, 768], P('fsdp', 'ctx')
- grad_proj_bias: float32 [768], P(('ctx', 'fsdp'))
- grad_second_gain: float32 [768], P(('ctx', 'fsdp'))
- grad_second_shift: float32 [768], P(('ctx', 'fsdp'))
- grad_fc_weight: float32 [768, 3072], P('fsdp', 'ctx')
- grad_fc_bias: float32 [3072], P(('ctx', 'fsdp'))
- grad_down_weight: float32 [3072, 768], P('fsdp', 'ctx')
- grad_down_bias: float32 [768], P(('ctx', 'fsdp'))
The draws below stay inside these ranges and needn't reach their ends.
Inputs may be any that keep to these rules, and one draw needn't show every extreme that they name: `block_order`: a permutation of 0 to 15.
All inputs are finite; a program needn't handle non-finite values.
Results may differ from the reference program's by a relative error of at most 0.033.
Values may be sent and summed in bfloat16 or wider, within the bound.
No kernel may reach another device: no remote copies, remote signals or barrier semaphores. Data moves between devices by JAX's collectives and lax.ppermute only.
A program may use at most 256 MiB of HBM per device.

```python
import math
import jax
import jax.numpy as jnp
from jax import lax

D = 768
H = 12
HD = 64
FF = 3072
BLK = 64
SEQS = 4
NBLK = 16
LEN = 1024


def draw_qkv_weight(key, part):
    base_key = jax.random.fold_in(jax.random.fold_in(key, 11), 0)
    standard = jnp.clip(jax.random.normal(base_key, (D, 3 * D), jnp.float32), -4.0, 4.0) / math.sqrt(D)
    return standard.astype(jnp.bfloat16)


def level_of(own_key, dims, pieces, smallest, top_value):
    def one(dim, shards_of):
        draws = jax.random.uniform(jax.random.fold_in(jax.random.fold_in(own_key, 6), dim), (shards_of,), jnp.float32, smallest / len(pieces), top_value / len(pieces))
        return jnp.repeat(jnp.exp(draws), dims[dim] // shards_of).reshape((-1,) + (1,) * (len(dims) - dim - 1))

    gain = one(*pieces[0])
    for cut in pieces[1:]:
        gain = gain * one(*cut)
    return gain


def scatter_about(stream_key, dims, spread, most, cuts=(), held_as=jnp.bfloat16):
    values = jax.random.normal(stream_key, dims, jnp.float32) * spread
    if len(cuts) > 0:
        values = level_of(stream_key, dims, cuts, -0.22, 0.18) * values
    return jnp.clip(values, min=-most, max=most).astype(held_as)


def setup_inputs(seed: int = 0) -> dict:
    splits = jax.random.split(jax.random.key(seed), 16)
    return {
        "inputs": scatter_about(splits[0], (SEQS, LEN, D), 1.0, 6.0, ((0, 4), (1, 8))),
        "block_order": jax.random.permutation(splits[1], NBLK).astype(jnp.int32),
        "cotangent": scatter_about(splits[2], (SEQS, LEN, D), 1.0, 6.0, ((0, 4), (1, 8))),
        "first_gain": jnp.clip(1.0 + 0.15 * jax.random.normal(splits[3], (D,), jnp.float32), 0.25, 1.75).astype(jnp.bfloat16),
        "first_shift": scatter_about(splits[4], (D,), 0.5, 3.0, ((0, 4),)),
        "qkv_weight": draw_qkv_weight(jax.random.fold_in(splits[15], 71), 0),
        "qv_bias": scatter_about(splits[6], (2 * D,), 0.5, 3.0, ((0, 4),)),
        "proj_weight": scatter_about(splits[7], (D, D), (D // 64) ** -0.5, 1.75, ((0, 4),)),
        "proj_bias": scatter_about(splits[8], (D,), 0.5, 3.0, ((0, 4),)),
        "second_gain": jnp.clip(1.0 + 0.15 * jax.random.normal(splits[9], (D,), jnp.float32), 0.25, 1.75).astype(jnp.bfloat16),
        "second_shift": scatter_about(splits[10], (D,), 0.5, 3.0, ((0, 4),)),
        "fc_weight": scatter_about(splits[11], (D, FF), D ** -0.5, 0.21875, ((0, 4),)),
        "fc_bias": scatter_about(splits[12], (FF,), 0.5, 3.0, ((0, 4),)),
        "down_weight": scatter_about(splits[13], (FF, D), FF ** -0.5, 0.109375, ((0, 4),)),
        "down_bias": scatter_about(splits[14], (D,), 0.5, 3.0, ((0, 4),)),
    }


epsilon = 1e-05
gelu_coeff = 0.7978845608028654

def split_heads(matrix):
    return matrix.reshape(matrix.shape[0], H, HD)

def norm_forward(rows_in, norm_gain, norm_shift):
    center = rows_in - lax.optimization_barrier(jnp.mean(rows_in, axis=-1, keepdims=True))
    inverse = lax.rsqrt(lax.optimization_barrier(jnp.mean(center * center, axis=-1, keepdims=True)) + epsilon)
    normed = center * inverse
    return (normed, inverse, (normed * norm_gain + norm_shift).astype(jnp.bfloat16))

def norm_backward(grad_out, normed, inverse, norm_gain):
    scaled = grad_out * norm_gain
    return inverse * (scaled - lax.optimization_barrier(jnp.mean(scaled, axis=-1, keepdims=True)) - normed * lax.optimization_barrier(jnp.mean(scaled * normed, axis=-1, keepdims=True)))

def gelu_pair(hidden_pre):
    argument = gelu_coeff * (hidden_pre + 0.044715 * hidden_pre * hidden_pre * hidden_pre)
    tangent = jnp.tanh(argument)
    result = 0.5 * hidden_pre * (1.0 + tangent)
    derivative = 0.5 * (1.0 + tangent) + 0.5 * hidden_pre * (1.0 - tangent * tangent) * gelu_coeff * (1.0 + 3.0 * 0.044715 * hidden_pre * hidden_pre)
    return (result, derivative)

def times_transposed(left_side, right_side):
    return lax.dot_general(left_side, right_side, (((1,), (1,)), ((), ())), preferred_element_type=jnp.float32)

def transposed_times(left_side, right_side):
    return lax.dot_general(left_side, right_side, (((0,), (0,)), ((), ())), preferred_element_type=jnp.float32)

def rounded(array):
    return lax.optimization_barrier(array.astype(jnp.bfloat16)).astype(jnp.float32)

def attention_forward(queries, key_rows, values, positions):
    block_width = min(512, LEN)
    scale_factor = 1.0 / math.sqrt(HD)
    key_heads = split_heads(key_rows).astype(jnp.float32)
    value_heads = split_heads(values).astype(jnp.float32)

    def one_block(first_row):
        query_heads = split_heads(lax.dynamic_slice_in_dim(queries, first_row, block_width, 0)).astype(jnp.float32)
        own_pos = lax.dynamic_slice_in_dim(positions, first_row, block_width, 0)
        visible = positions[None, :] <= own_pos[:, None]
        scores = jnp.einsum('qhd,khd->hqk', query_heads, key_heads, precision=lax.Precision.HIGHEST) * scale_factor
        scores = jnp.where(visible[None], scores, -jnp.inf)
        largest = lax.optimization_barrier(jnp.max(scores, axis=2))
        log_total = largest + jnp.log(lax.optimization_barrier(jnp.sum(jnp.exp(scores - largest[:, :, None]), axis=2)))
        weights = rounded(jnp.exp(scores - log_total[:, :, None]))
        attended = jnp.einsum('hqk,khd->qhd', weights, value_heads, precision=lax.Precision.HIGHEST)
        return (attended.reshape(block_width, D).astype(jnp.bfloat16), log_total.T)
    starts = jnp.arange(LEN // block_width, dtype=jnp.int32) * block_width
    attended, lse_rows = lax.map(one_block, starts)
    return (attended.reshape(LEN, D), lse_rows.reshape(LEN, H))

def attention_backward(queries, key_rows, values, attended_grad, lse_rows, delta_rows, positions):
    block_width = min(512, LEN)
    scale_factor = 1.0 / math.sqrt(HD)
    key_heads = split_heads(key_rows).astype(jnp.float32)
    value_heads = split_heads(values).astype(jnp.float32)

    def one_block(carry, first_row):
        key_total, value_total = carry
        query_heads = split_heads(lax.dynamic_slice_in_dim(queries, first_row, block_width, 0)).astype(jnp.float32)
        grad_heads = split_heads(lax.dynamic_slice_in_dim(attended_grad, first_row, block_width, 0)).astype(jnp.float32)
        lse_block = lax.dynamic_slice_in_dim(lse_rows, first_row, block_width, 0).T
        delta_block = lax.dynamic_slice_in_dim(delta_rows, first_row, block_width, 0).T
        own_pos = lax.dynamic_slice_in_dim(positions, first_row, block_width, 0)
        visible = positions[None, :] <= own_pos[:, None]
        scores = jnp.einsum('qhd,khd->hqk', query_heads, key_heads, precision=lax.Precision.HIGHEST) * scale_factor
        probs = jnp.where(visible[None], jnp.exp(scores - lse_block[:, :, None]), 0.0)
        prob_grad = jnp.einsum('qhd,khd->hqk', grad_heads, value_heads, precision=lax.Precision.HIGHEST)
        score_grad = rounded(probs * (prob_grad - delta_block[:, :, None]))
        weights = rounded(probs)
        query_grad = jnp.einsum('hqk,khd->qhd', score_grad, key_heads, precision=lax.Precision.HIGHEST) * scale_factor
        key_total = key_total + jnp.einsum('hqk,qhd->khd', score_grad, query_heads, precision=lax.Precision.HIGHEST) * scale_factor
        value_total = value_total + jnp.einsum('hqk,qhd->khd', weights, grad_heads, precision=lax.Precision.HIGHEST)
        return ((key_total, value_total), query_grad.reshape(block_width, D))
    zero_heads = jnp.zeros((LEN, H, HD), jnp.float32)
    starts = jnp.arange(LEN // block_width, dtype=jnp.int32) * block_width
    (key_total, value_total), query_grad = lax.scan(one_block, (zero_heads, zero_heads), starts)
    return (query_grad.reshape(LEN, D), key_total.reshape(LEN, D), value_total.reshape(LEN, D))

def reference(inputs, block_order, cotangent, first_gain, first_shift, qkv_weight, qv_bias, proj_weight, proj_bias, second_gain, second_shift, fc_weight, fc_bias, down_weight, down_bias):
    positions = (block_order[:, None] * BLK + jnp.arange(BLK, dtype=jnp.int32)[None, :]).reshape(LEN).astype(jnp.int32)

    def one_sequence(totals, sequence_pair):
        tokens_in, upstream = sequence_pair
        tokens = tokens_in.astype(jnp.float32)
        first_normed, first_inverse, first_hidden = norm_forward(tokens, first_gain, first_shift)
        projected = jnp.dot(first_hidden, qkv_weight, preferred_element_type=jnp.float32)
        queries = (projected[:, :D] + qv_bias[:D]).astype(jnp.bfloat16)
        key_rows = projected[:, D:2 * D].astype(jnp.bfloat16)
        values = (projected[:, 2 * D:] + qv_bias[D:]).astype(jnp.bfloat16)
        attended, lse_rows = attention_forward(queries, key_rows, values, positions)
        residual = tokens + jnp.dot(attended, proj_weight, preferred_element_type=jnp.float32) + proj_bias
        second_normed, second_inverse, second_hidden = norm_forward(residual, second_gain, second_shift)
        hidden_pre = jnp.dot(second_hidden, fc_weight, preferred_element_type=jnp.float32) + fc_bias
        activation, derivative = gelu_pair(hidden_pre)
        activation_b = activation.astype(jnp.bfloat16)
        block_out = (residual + jnp.dot(activation_b, down_weight, preferred_element_type=jnp.float32) + down_bias).astype(jnp.bfloat16)
        upstream_f = upstream.astype(jnp.float32)
        down_wgrad = transposed_times(activation_b, upstream)
        down_bgrad = lax.optimization_barrier(jnp.sum(upstream_f, axis=0))
        pre_grad = times_transposed(upstream, down_weight) * derivative
        pre_grad_b = pre_grad.astype(jnp.bfloat16)
        fc_wgrad = transposed_times(second_hidden, pre_grad_b)
        fc_bgrad = lax.optimization_barrier(jnp.sum(pre_grad, axis=0))
        second_grad = times_transposed(pre_grad_b, fc_weight)
        second_ggrad = lax.optimization_barrier(jnp.sum(second_grad * second_normed, axis=0))
        second_sgrad = lax.optimization_barrier(jnp.sum(second_grad, axis=0))
        residual_grad = upstream_f + norm_backward(second_grad, second_normed, second_inverse, second_gain)
        residual_grad_b = residual_grad.astype(jnp.bfloat16)
        proj_wgrad = transposed_times(attended, residual_grad_b)
        proj_bgrad = lax.optimization_barrier(jnp.sum(residual_grad, axis=0))
        attended_grad = times_transposed(residual_grad_b, proj_weight).astype(jnp.bfloat16)
        delta_rows = jnp.einsum('qhd,qhd->qh', split_heads(attended_grad).astype(jnp.float32), split_heads(attended).astype(jnp.float32), precision=lax.Precision.HIGHEST)
        query_grad, key_grad, value_grad = attention_backward(queries, key_rows, values, attended_grad, lse_rows, delta_rows, positions)
        qkv_grad = jnp.concatenate([query_grad, key_grad, value_grad], axis=1).astype(jnp.bfloat16)
        qkv_wgrad = transposed_times(first_hidden, qkv_grad)
        qv_bgrad = jnp.concatenate([lax.optimization_barrier(jnp.sum(query_grad, axis=0)), lax.optimization_barrier(jnp.sum(value_grad, axis=0))])
        first_grad = times_transposed(qkv_grad, qkv_weight)
        first_ggrad = lax.optimization_barrier(jnp.sum(first_grad * first_normed, axis=0))
        first_sgrad = lax.optimization_barrier(jnp.sum(first_grad, axis=0))
        input_grad = residual_grad + norm_backward(first_grad, first_normed, first_inverse, first_gain)
        gradients = (first_ggrad, first_sgrad, qkv_wgrad, qv_bgrad, proj_wgrad, proj_bgrad, second_ggrad, second_sgrad, fc_wgrad, fc_bgrad, down_wgrad, down_bgrad)
        return (jax.tree.map(jnp.add, totals, gradients), (block_out, input_grad))
    start_totals = (jnp.zeros((D,), jnp.float32), jnp.zeros((D,), jnp.float32), jnp.zeros((D, 3 * D), jnp.float32), jnp.zeros((2 * D,), jnp.float32), jnp.zeros((D, D), jnp.float32), jnp.zeros((D,), jnp.float32), jnp.zeros((D,), jnp.float32), jnp.zeros((D,), jnp.float32), jnp.zeros((D, FF), jnp.float32), jnp.zeros((FF,), jnp.float32), jnp.zeros((FF, D), jnp.float32), jnp.zeros((D,), jnp.float32))
    totals, (block_out, grad_input) = lax.scan(one_sequence, start_totals, (inputs, cotangent))
    return (block_out, grad_input, totals[0], totals[1], totals[2], totals[3], totals[4], totals[5], totals[6], totals[7], totals[8], totals[9], totals[10], totals[11])
```

```python
import math

import numpy as np

import jax
import jax.numpy as jnp
from jax import lax
from jax.sharding import PartitionSpec as P

HD = 64

epsilon = 1e-05
negative_big = -1e30
gelu_coeff = 0.7978845608028654
bf16 = jnp.bfloat16
f32 = jnp.float32


def swap(value, axis, mask):
    count = lax.axis_size(axis)
    return lax.ppermute(value, axis, [(i, i ^ mask) for i in range(count)])


def bits_of(count):
    return count.bit_length() - 1


def normalize(rows):
    center = rows - jnp.mean(rows, axis=-1, keepdims=True)
    inverse = lax.rsqrt(jnp.mean(center * center, axis=-1, keepdims=True) + epsilon)
    return center * inverse, inverse


def norm_backward(grad_out, normed, inverse, gain):
    scaled = grad_out * gain
    return inverse * (
        scaled
        - jnp.mean(scaled, axis=-1, keepdims=True)
        - normed * jnp.mean(scaled * normed, axis=-1, keepdims=True)
    )


def gelu_pair(hidden_pre):
    argument = gelu_coeff * (hidden_pre + 0.044715 * hidden_pre * hidden_pre * hidden_pre)
    tangent = jnp.tanh(argument)
    result = 0.5 * hidden_pre * (1.0 + tangent)
    derivative = 0.5 * (1.0 + tangent) + 0.5 * hidden_pre * (
        1.0 - tangent * tangent
    ) * gelu_coeff * (1.0 + 3.0 * 0.044715 * hidden_pre * hidden_pre)
    return (result, derivative)


def dotf(spec, left, right):
    return jnp.einsum(spec, left, right, preferred_element_type=f32)


def positions_of(block_order, owners, rows_dev, block_rows):
    per_dev = rows_dev // block_rows
    row = jnp.arange(rows_dev, dtype=jnp.int32)
    stored = owners[:, None] * per_dev + (row // block_rows)[None, :]
    matches = stored[:, :, None] == jnp.arange(block_order.shape[0], dtype=jnp.int32)
    blocks = jnp.sum(jnp.where(matches, block_order, 0), axis=2)
    return blocks * block_rows + (row % block_rows)[None, :]


def matchings(edges, count, degree):
    left = [[] for _ in range(count)]
    for edge in edges:
        left[edge[0]].append(edge)
    rounds = []
    for _ in range(degree):
        owner = {}

        def place(source, seen):
            for edge in left[source]:
                if edge[1] in seen:
                    continue
                seen.add(edge[1])
                if edge[1] not in owner or place(owner[edge[1]][0], seen):
                    owner[edge[1]] = edge
                    return True
            return False

        for source in range(count):
            place(source, set())
        picked = sorted(owner.values())
        for edge in picked:
            left[edge[0]].remove(edge)
        rounds.append(picked)
    return rounds


def halve(low, high, bit, mask):
    keep = jnp.where(bit == 0, low, high)
    send = jnp.where(bit == 0, high, low).astype(bf16)
    return keep + swap(send, "ctx", mask).astype(f32)


def sum_over_fsdp(partial):
    count = lax.axis_size("fsdp")
    half = count // 2
    total = partial[:half] + swap(partial[half:].astype(bf16), "fsdp", 1).astype(f32)
    for b in range(bits_of(half)):
        step = 1 << b
        kept = total.astype(bf16)
        other = swap(kept, "fsdp", half >> b)
        order = [i ^ step for i in range(half)]
        total = kept.astype(f32) + jnp.stack([other[i] for i in order]).astype(f32)
    return total


def to_owner(partial):
    count = lax.axis_size("fsdp")
    held = partial
    mask = 1
    while held.shape[0] > 1:
        half = held.shape[0] // 2
        held = held[:half] + swap(held[half:].astype(bf16), "fsdp", mask).astype(f32)
        mask *= 2
    return held[0]


def gather_fsdp(value):
    held = value[None]
    mask = lax.axis_size("fsdp") // 2
    while mask:
        held = jnp.concatenate([held, swap(held, "fsdp", mask)], axis=0)
        mask //= 2
    return held


def reversed_bits(value, count):
    result = value * 0
    for b in range(bits_of(count)):
        result = result + ((value >> b) & 1) * (count >> (b + 1))
    return result


def columns_for_all(pieces):
    count, rows, width = pieces.shape
    me = lax.axis_index("fsdp")
    held = jnp.zeros((count, rows, width), pieces.dtype)
    for k in range(count):
        piece = lax.dynamic_index_in_dim(pieces, me ^ k, 0, keepdims=False)
        if k:
            piece = swap(piece, "fsdp", k)
        held = lax.dynamic_update_index_in_dim(held, piece, me ^ k, 0)
    return held.reshape(count * rows, width)


def on_device(
    inputs,
    block_order,
    cotangent,
    first_gain,
    first_shift,
    qkv_weight,
    qv_bias,
    proj_weight,
    proj_bias,
    second_gain,
    second_shift,
    fc_weight,
    fc_bias,
    down_weight,
    down_bias,
):
    nctx = lax.axis_size("ctx")
    nf = lax.axis_size("fsdp")
    c = lax.axis_index("ctx")
    f = lax.axis_index("fsdp")
    _, rows_dev, width = inputs.shape
    piece = width // nf
    heads = piece // HD
    ff = down_weight.shape[0]
    block_rows = rows_dev * nctx // block_order.shape[0]
    group = nctx // nf
    s, g = c // group, c % group
    scale = 1.0 / math.sqrt(HD)

    vectors = jnp.concatenate(
        [first_gain, first_shift, proj_bias, second_gain, second_shift, down_bias, qv_bias]
    ).reshape(-1, 128)
    tokens_b = gather_fsdp(inputs[0])
    vectors_all = gather_fsdp(vectors).reshape(nf, 8, piece).astype(f32)
    w_qkv = columns_for_all(
        qkv_weight.reshape(piece, 3, nf, piece).transpose(2, 0, 1, 3).reshape(nf, piece, 3 * piece)
    )
    upstream = gather_fsdp(cotangent[0])
    w_fc = columns_for_all(fc_weight.reshape(piece, nf, ff).transpose(1, 0, 2))

    owner_of = jnp.arange(nf, dtype=jnp.int32)
    slot_of = reversed_bits(owner_of ^ f, nf)
    pick = slot_of[:, None] == owner_of[None, :]
    in_order = jnp.sum(
        jnp.where(pick[:, :, None, None], vectors_all[None], 0.0), axis=1
    )
    flat = in_order[:, :6].transpose(1, 0, 2).reshape(6, width)
    gain1, shift1, pbias, gain2, shift2, dbias = (flat[i] for i in range(6))
    qv_flat = in_order[:, 6:].reshape(2, nf, piece)
    mine = (owner_of == f)[None, :, None]
    qv_mine = jnp.sum(jnp.where(mine, qv_flat, 0.0), axis=1)
    bias_rows = jnp.concatenate([qv_mine[0], jnp.zeros((piece,), f32), qv_mine[1]])

    tokens = tokens_b.astype(f32)
    normed1, inverse1 = normalize(tokens)
    hidden1 = (normed1 * gain1 + shift1).astype(bf16)
    qkv_t = (dotf("ef,pte->pft", w_qkv, hidden1) + bias_rows[None, :, None]).astype(bf16)

    def spread(blocks):
        out = []
        for j in range(nf):
            block = lax.dynamic_index_in_dim(blocks, s ^ j, 0, keepdims=False)
            out.append(swap(block, "ctx", j * group) if j else block)
        return jnp.stack(out)

    def collect(blocks):
        out = jnp.zeros(blocks.shape, blocks.dtype)
        for j in range(nf):
            block = swap(blocks[j], "ctx", j * group) if j else blocks[j]
            out = lax.dynamic_update_index_in_dim(out, block, s ^ j, 0)
        return out

    kv_blocks = spread(qkv_t[:, piece:])
    q_blocks = spread(qkv_t[:, :piece])
    kv_all = kv_blocks[None]
    mask = group // 2
    while mask:
        kv_all = jnp.concatenate([kv_all, swap(kv_all, "ctx", mask)], axis=0)
        mask //= 2
    members = reversed_bits(jnp.arange(group, dtype=jnp.int32), group) ^ g
    own_group = s ^ owner_of
    q_pos = positions_of(block_order, own_group * group + g, rows_dev, block_rows).reshape(-1)
    k_pos = positions_of(
        block_order,
        (own_group[None, :] * group + members[:, None]).reshape(-1),
        rows_dev,
        block_rows,
    ).reshape(-1)
    nq, nk = nf * rows_dev, nctx * rows_dev
    to_lanes = lambda a: a.transpose(1, 0, 2).reshape(heads, HD, -1)
    q_t = to_lanes(q_blocks)
    kv_flat = kv_all.reshape(nctx, 2 * piece, rows_dev)
    k_t = to_lanes(kv_flat[:, :piece])
    v_t = to_lanes(kv_flat[:, piece:])
    visible = (k_pos[:, None] <= q_pos[None, :])[None]
    scores = jnp.where(visible, dotf("hdk,hdq->hkq", k_t, q_t) * scale, negative_big)
    largest = jnp.max(scores, axis=1, keepdims=True)
    raised = jnp.exp(scores - largest)
    weights = (raised * (1.0 / jnp.sum(raised, axis=1, keepdims=True))).astype(bf16)
    att_t = dotf("hdk,hkq->hdq", v_t, weights).astype(bf16)
    att_blocks = att_t.reshape(piece, nf, rows_dev).transpose(1, 0, 2)
    att = collect(att_blocks)

    half = nf // 2
    total = sum_over_fsdp(dotf("pft,fo->pto", att, proj_weight))
    residual = tokens[:half] + total + pbias
    normed2, inverse2 = normalize(residual)
    hidden2_half = (normed2 * gain2 + shift2).astype(bf16)
    hidden2 = jnp.concatenate([hidden2_half, swap(hidden2_half, "fsdp", 1)], axis=0)
    rows_all = nf * rows_dev
    hidden2 = hidden2.reshape(rows_all, width)
    hidden_pre = dotf("te,eh->th", hidden2, w_fc) + fc_bias.astype(f32)
    activation, derivative = gelu_pair(hidden_pre)
    activation_b = activation.astype(bf16)
    up_rows = upstream.reshape(rows_all, width)
    pre_grad = dotf("to,ho->th", up_rows, down_weight) * derivative
    pre_grad_b = pre_grad.astype(bf16)
    second_grad = sum_over_fsdp(
        dotf("th,eh->te", pre_grad_b, w_fc).reshape(nf, rows_dev, width)
    )
    up_half = upstream[:half].astype(f32)
    residual_grad = up_half + norm_backward(second_grad, normed2, inverse2, gain2)
    rgrad_half = residual_grad.astype(bf16)
    rgrad = jnp.concatenate([rgrad_half, swap(rgrad_half, "fsdp", 1)], axis=0)
    agrad = dotf("fo,pto->pft", proj_weight, rgrad).astype(bf16)

    do_t = to_lanes(spread(agrad))
    delta = jnp.sum(do_t.astype(f32) * att_t.astype(f32), axis=1, keepdims=True)
    prob_grad = dotf("hdk,hdq->hkq", v_t, do_t)
    score_grad = (weights.astype(f32) * (prob_grad - delta)).astype(bf16)
    dv_t = dotf("hdq,hkq->hdk", do_t, weights)
    dk_t = dotf("hdq,hkq->hdk", q_t, score_grad) * scale
    dq_t = (dotf("hdk,hkq->hdq", k_t, score_grad) * scale).astype(bf16)
    dkv = jnp.concatenate([dk_t.reshape(piece, -1), dv_t.reshape(piece, -1)], axis=0)
    dkv = dkv.reshape(2 * piece, nctx, rows_dev).transpose(1, 0, 2)
    dkv = dkv.reshape(group, nf, 2 * piece, rows_dev)
    mask = 1
    while dkv.shape[0] > 1:
        h = dkv.shape[0] // 2
        dkv = dkv[:h] + swap(dkv[h:].astype(bf16), "ctx", mask).astype(f32)
        mask *= 2
    dq_blocks = dq_t.reshape(piece, nf, rows_dev).transpose(1, 0, 2)
    dq_own = collect(dq_blocks)
    dkv_own = collect(dkv[0].astype(bf16))
    qkv_grad = jnp.concatenate([dq_own, dkv_own], axis=1)

    first_part = dotf("pft,ef->pte", qkv_grad, w_qkv)
    g_qkv = dotf("pft,pte->fe", qkv_grad, hidden1)
    first_grad = to_owner(first_part)
    input_grad = residual_grad[0] + norm_backward(first_grad, normed1[0], inverse1[0], gain1)

    block_out = residual[0] + to_owner(
        dotf("th,ho->to", activation_b, down_weight).reshape(nf, rows_dev, width)
    ) + dbias

    nbits = bits_of(nctx)
    bit = [(c >> b) & 1 for b in range(nbits)]

    def rows_scatter(value):
        held = value.reshape((2,) * nbits + (value.shape[0] // nctx,) + value.shape[1:])
        for b in range(nbits):
            at = (slice(None),) * (nbits - 1 - b)
            held = halve(held[at + (0,)], held[at + (1,)], bit[b], 1 << b)
        return held

    g_down = rows_scatter(dotf("to,th->oh", up_rows, activation_b)).T
    g_proj = rows_scatter(dotf("pto,pft->of", rgrad, att)).T

    held = dotf("te,th->eh", hidden2, pre_grad_b)
    gbits = bits_of(group)
    for b in reversed(range(gbits)):
        w = held.shape[1] // 2
        held = halve(held[:, :w], held[:, w:], bit[b], 1 << b)
    sbits = bits_of(nf)
    held = held.reshape((2,) * sbits + (piece, held.shape[1]))
    for b in range(sbits):
        at = (slice(None),) * (sbits - 1 - b)
        held = halve(held[at + (0,)], held[at + (1,)], bit[gbits + b], 1 << (gbits + b))
    pairs = []
    for cc in range(nctx):
        for fi in range(nf):
            pairs.append((cc * nf + fi, (fi * group + cc % group) * nf + cc // group))
    g_fc = lax.ppermute(held.astype(bf16), ("ctx", "fsdp"), pairs).astype(f32)

    held = g_qkv
    for b in range(sbits):
        w = held.shape[1] // 2
        held = halve(held[:, :w], held[:, w:], bit[b], 1 << b)
    held = held.reshape((2,) * (nbits - sbits) + (-1, piece))
    for b in range(sbits, nbits):
        at = (slice(None),) * (nbits - 1 - b)
        held = halve(held[at + (0,)], held[at + (1,)], bit[b], 1 << b)
    unit = width // nctx
    edges = []
    for cc in range(nctx):
        r = sum(((cc >> b) & 1) * (nf >> (b + 1)) for b in range(sbits))
        for fi in range(nf):
            for e in range(3):
                row = ((cc >> sbits) * 3 + e) * unit
                column = (row // piece) * width + fi * piece + row % piece
                target = (column // (3 * unit)) * nf + r
                edges.append((cc * nf + fi, target, (e, (column % (3 * unit)) // unit)))
    device = c * nf + f
    units = held.astype(bf16).reshape(3, unit, piece)
    got = jnp.zeros((3, unit, piece), bf16)
    for chosen in matchings(edges, nctx * nf, 3):
        which = np.zeros((nctx * nf,), np.int32)
        slot = np.zeros((nctx * nf,), np.int32)
        for source, target, (e, place) in chosen:
            which[source] = e
            slot[target] = place
        sent = lax.dynamic_index_in_dim(units, jnp.asarray(which)[device], 0, keepdims=False)
        came = lax.ppermute(sent, ("ctx", "fsdp"), [(a, b) for a, b, _ in chosen])
        got = lax.dynamic_update_index_in_dim(got, came, jnp.asarray(slot)[device], 0)
    g_qkv_own = got.reshape(3 * unit, piece).T.astype(f32)

    def sum_ctx(value):
        for b in range(nbits):
            value = value + swap(value, "ctx", 1 << b)
        return value

    early = jnp.stack(
        [
            jnp.sum(up_half, axis=(0, 1)),
            jnp.sum(residual_grad, axis=(0, 1)),
            jnp.sum(second_grad * normed2, axis=(0, 1)),
            jnp.sum(second_grad, axis=(0, 1)),
        ]
    )
    early = jnp.concatenate([early, jnp.sum(pre_grad, axis=0).reshape(-1, width)], axis=0)
    early = sum_ctx(early)
    other = swap(early, "fsdp", 1)
    summed = early[:4] + other[:4]
    fc_sums = jnp.stack([early[4:].reshape(-1), other[4:].reshape(-1)])
    late = jnp.concatenate(
        [
            jnp.sum(first_part * normed1, axis=(0, 1)),
            jnp.sum(first_part, axis=(0, 1)),
            jnp.sum(qkv_grad[:, :piece].astype(f32), axis=(0, 2)),
            jnp.sum(qkv_grad[:, 2 * piece :].astype(f32), axis=(0, 2)),
        ]
    )
    late = sum_ctx(late.reshape(-1, 128)).reshape(-1)
    first_sums, qv_sums = late[: 2 * width], late[2 * width :][None]
    first_sums = first_sums + swap(first_sums, "fsdp", 1)
    qv_sums = jnp.concatenate([qv_sums, swap(qv_sums, "fsdp", 1)], axis=0)
    mask = 2
    while mask < nf:
        first_sums = first_sums + swap(first_sums, "fsdp", mask)
        qv_sums = jnp.concatenate([qv_sums, swap(qv_sums, "fsdp", mask)], axis=0)
        fc_sums = jnp.concatenate([fc_sums, swap(fc_sums, "fsdp", mask)], axis=0)
        mask *= 2

    size = width // (nctx * nf)
    six = jnp.concatenate([summed, first_sums.reshape(2, width)], axis=0)
    own = lax.dynamic_slice_in_dim(six, device * size, size, 1)
    start = device * 2 * size
    part, rest = start // width, start % width
    qv_own = lax.dynamic_slice_in_dim(
        qv_sums.reshape(-1),
        (((rest // piece) ^ f) * 2 + part) * piece + rest % piece,
        2 * size,
        0,
    )
    fsize = ff // nctx
    start = device * fsize
    fc_own = lax.dynamic_slice_in_dim(
        fc_sums.reshape(-1), ((start // ff) ^ f) * ff + start % ff, fsize, 0
    )
    return (
        block_out.astype(bf16)[None],
        input_grad[None],
        own[4],
        own[5],
        g_qkv_own,
        qv_own,
        g_proj,
        own[1],
        own[2],
        own[3],
        g_fc,
        fc_own,
        g_down,
        own[0],
    )


def solution(mesh):
    vector, matrix = P("fsdp"), P("fsdp", None)
    placed = (
        P("fsdp", "ctx", None),
        P(),
        P("fsdp", "ctx", None),
        vector,
        vector,
        matrix,
        vector,
        matrix,
        vector,
        vector,
        vector,
        matrix,
        vector,
        matrix,
        vector,
    )
    spread, block = P(("ctx", "fsdp")), P("fsdp", "ctx")
    return jax.shard_map(
        on_device,
        mesh=mesh,
        in_specs=placed,
        out_specs=(
            P("fsdp", "ctx", None),
            P("fsdp", "ctx", None),
            spread,
            spread,
            block,
            spread,
            block,
            spread,
            spread,
            spread,
            block,
            spread,
            block,
            spread,
        ),
        check_vma=False,
    )
```

```python
import functools
import math

import jax
import jax.numpy as jnp
from jax import lax
from jax.experimental import pallas as pl
from jax.experimental.pallas import tpu as pltpu
from jax.sharding import PartitionSpec as P

HD = 64

epsilon = 1e-05
negative_big = -1e30
gelu_coeff = 0.7978845608028654
bf16 = jnp.bfloat16
f32 = jnp.float32


def swap(value, axis, mask):
    count = lax.axis_size(axis)
    return lax.ppermute(value, axis, [(i, i ^ mask) for i in range(count)])


def bits_of(count):
    return count.bit_length() - 1


def normalize(rows):
    center = rows - jnp.mean(rows, axis=-1, keepdims=True)
    inverse = lax.rsqrt(jnp.mean(center * center, axis=-1, keepdims=True) + epsilon)
    return center * inverse, inverse


def norm_backward(grad_out, normed, inverse, gain):
    scaled = grad_out * gain
    return inverse * (
        scaled
        - jnp.mean(scaled, axis=-1, keepdims=True)
        - normed * jnp.mean(scaled * normed, axis=-1, keepdims=True)
    )


def gelu_pair(hidden_pre):
    argument = gelu_coeff * (hidden_pre + 0.044715 * hidden_pre * hidden_pre * hidden_pre)
    tangent = jnp.tanh(argument)
    result = 0.5 * hidden_pre * (1.0 + tangent)
    derivative = 0.5 * (1.0 + tangent) + 0.5 * hidden_pre * (
        1.0 - tangent * tangent
    ) * gelu_coeff * (1.0 + 3.0 * 0.044715 * hidden_pre * hidden_pre)
    return (result, derivative)


def dotf(spec, left, right):
    return jnp.einsum(spec, left, right, preferred_element_type=f32)


def positions_of(block_order, owners, rows_dev, block_rows):
    per_dev = rows_dev // block_rows
    row = jnp.arange(rows_dev, dtype=jnp.int32)
    stored = owners[:, None] * per_dev + (row // block_rows)[None, :]
    matches = stored[:, :, None] == jnp.arange(block_order.shape[0], dtype=jnp.int32)
    blocks = jnp.sum(jnp.where(matches, block_order, 0), axis=2)
    return blocks * block_rows + (row % block_rows)[None, :]


def after(value, *others):
    return lax.optimization_barrier((value,) + others)[0]


def whole(count):
    return [pl.BlockSpec(memory_space=pltpu.VMEM)] * count


def kernel_call(kernel, outs, scalars, operands, scratch=(), cost=0):
    smem = [pl.BlockSpec(memory_space=pltpu.SMEM)] * len(scalars)
    return pl.pallas_call(
        kernel,
        out_shape=[jax.ShapeDtypeStruct(shape, dtype) for shape, dtype in outs],
        in_specs=smem + whole(len(operands)),
        out_specs=whole(len(outs)),
        scratch_shapes=list(scratch),
        compiler_params=pltpu.CompilerParams(vmem_limit_bytes=60 * 1024 * 1024),
        cost_estimate=pl.CostEstimate(flops=cost, bytes_accessed=1 << 20, transcendentals=0),
    )(*scalars, *operands)


def contract(left, right, dims):
    return lax.dot_general(left, right, ((dims[0], dims[1]), ((), ())), preferred_element_type=f32)


def cut_qkv_kernel(me_ref, w_ref, *outs):
    count = len(outs)
    piece = outs[0].shape[1] // 3
    me = me_ref[0]
    for t in range(count):
        for k in range(count):

            @pl.when((me ^ k) == t)
            def _():
                for part in range(3):
                    start = (part * count + t) * piece
                    outs[k][:, part * piece : (part + 1) * piece] = w_ref[:, start : start + piece]


def cut_fc_kernel(me_ref, w_ref, *outs):
    ff = outs[0].shape[1]
    for k in range(len(outs)):
        start = pl.multiple_of((me_ref[0] ^ k) * ff, 128)
        outs[k][...] = w_ref[:, pl.ds(start, ff)]


def join_kernel(me_ref, *refs):
    rows = refs[0].shape[0]
    for k, ref in enumerate(refs[:-1]):
        refs[-1][pl.ds(pl.multiple_of((me_ref[0] ^ k) * rows, rows), rows), :] = ref[...]


def project_kernel(nf, at_ref, own_ref, *refs):
    x_refs, (gain_ref, shift_ref, bias_ref) = refs[:nf], refs[nf : nf + 3]
    w_refs = refs[nf + 3 : 2 * nf + 2]
    w_refs = (own_ref,) + w_refs
    q_refs = refs[2 * nf + 2 : 3 * nf + 2]
    kv_refs = refs[3 * nf + 2 : 4 * nf + 2]
    hidden_ref, normed_ref, w_out, x_scr = refs[4 * nf + 2 :]
    me, group = at_ref[0], at_ref[1]
    piece = own_ref.shape[0]
    for k in range(nf):
        w_out[pl.ds(pl.multiple_of((me ^ k) * piece, piece), piece), :] = w_refs[k][...]
        x_scr[k] = x_refs[k][...]
    for j in range(nf):
        rows = x_scr[group ^ j].astype(f32)
        normed, _ = normalize(rows)
        hidden = (normed * gain_ref[...] + shift_ref[...]).astype(bf16)
        normed_ref[group ^ j] = normed
        hidden_ref[group ^ j] = hidden
        result = contract(hidden, w_out[...], ((1,), (0,))) + bias_ref[...]
        turned = result.T.astype(bf16)
        q_refs[j][...] = turned[:piece]
        kv_refs[j][...] = turned[piece:]


def attend_kernel(nf, members, block_rows, heads, kb_ref, qpos_ref, *refs):
    q_refs, kv_refs = refs[:nf], refs[nf : nf + members]
    p_ref = refs[nf + members]
    o_refs = refs[nf + members + 1 : nf + members + 1 + nf]
    s_scr = refs[-1]
    rows = kv_refs[0].shape[1]
    qpos = qpos_ref[...]
    scale = 1.0 / math.sqrt(HD)

    def one_head(h, carry):
        at = pl.ds(pl.multiple_of(h * HD, HD), HD)
        at_v = pl.ds(pl.multiple_of((heads + h) * HD, HD), HD)
        q = jnp.concatenate([ref[at, :] for ref in q_refs], axis=1)
        largest = jnp.full((1, q.shape[1]), negative_big, f32)
        for i in range(members):
            scores = contract(kv_refs[i][at, :], q, ((0,), (0,))) * scale
            for b in range(rows // block_rows):
                part = scores[b * block_rows : (b + 1) * block_rows]
                pos = kb_ref[i * (rows // block_rows) + b] * block_rows
                pos = pos + lax.broadcasted_iota(jnp.int32, part.shape, 0)
                part = jnp.where(pos <= qpos, part, negative_big)
                start = i * rows + b * block_rows
                s_scr[start : start + block_rows, :] = part
                largest = jnp.maximum(largest, jnp.max(part, axis=0, keepdims=True))
        total = jnp.zeros_like(largest)
        for i in range(members):
            raised = jnp.exp(s_scr[i * rows : (i + 1) * rows, :] - largest)
            s_scr[i * rows : (i + 1) * rows, :] = raised
            total = total + jnp.sum(raised, axis=0, keepdims=True)
        inverse = 1.0 / total
        mixed = jnp.zeros((HD, q.shape[1]), f32)
        for i in range(members):
            weights = (s_scr[i * rows : (i + 1) * rows, :] * inverse).astype(bf16)
            p_ref[h, i * rows : (i + 1) * rows, :] = weights
            mixed = mixed + contract(kv_refs[i][at_v, :], weights, ((1,), (0,)))
        mixed = mixed.astype(bf16)
        for j in range(nf):
            o_refs[j][at, :] = mixed[:, j * rows : (j + 1) * rows]
        return carry

    lax.fori_loop(0, heads, one_head, 0)


def attend_back_kernel(nf, members, heads, p_ref, *refs):
    q_refs, do_refs, o_refs = refs[:nf], refs[nf : 2 * nf], refs[2 * nf : 3 * nf]
    kv_refs = refs[3 * nf : 3 * nf + members]
    dq_refs = refs[3 * nf + members : 4 * nf + members]
    dkv_refs = refs[4 * nf + members :]
    rows = kv_refs[0].shape[1]
    scale = 1.0 / math.sqrt(HD)

    def one_head(h, carry):
        at = pl.ds(pl.multiple_of(h * HD, HD), HD)
        at_v = pl.ds(pl.multiple_of((heads + h) * HD, HD), HD)
        q = jnp.concatenate([ref[at, :] for ref in q_refs], axis=1)
        do = jnp.concatenate([ref[at, :] for ref in do_refs], axis=1)
        o = jnp.concatenate([ref[at, :] for ref in o_refs], axis=1)
        delta = jnp.sum(do.astype(f32) * o.astype(f32), axis=0, keepdims=True)
        dq = jnp.zeros(q.shape, f32)
        for i in range(members):
            weights = p_ref[h, i * rows : (i + 1) * rows, :]
            prob_grad = contract(kv_refs[i][at_v, :], do, ((0,), (0,)))
            score_grad = (weights.astype(f32) * (prob_grad - delta)).astype(bf16)
            kind = dkv_refs[i].dtype
            dkv_refs[i][at_v, :] = contract(do, weights, ((1,), (1,))).astype(kind)
            dkv_refs[i][at, :] = (contract(q, score_grad, ((1,), (1,))) * scale).astype(kind)
            dq = dq + contract(kv_refs[i][at, :], score_grad, ((1,), (0,)))
        dq = (dq * scale).astype(bf16)
        for j in range(nf):
            dq_refs[j][at, :] = dq[:, j * rows : (j + 1) * rows]
        return carry

    lax.fori_loop(0, heads, one_head, 0)


def begin(halves, bit, mask):
    low, high = halves
    return jnp.where(bit == 0, low, high), jnp.where(bit == 0, high, low).astype(bf16)


def finish(keep, send, mask, point=None):
    came = swap(send, "ctx", mask)
    if point is not None:
        came = after(came, point)
    return keep + came.astype(f32)


def halve(halves, bit, mask, point=None):
    return finish(*begin(halves, bit, mask), mask, point)


def sum_over_fsdp(partial, meanwhile=None):
    count = lax.axis_size("fsdp")
    half = count // 2
    total = partial[:half] + swap(partial[half:].astype(bf16), "fsdp", 1).astype(f32)
    for b in range(bits_of(half)):
        step = 1 << b
        kept = total.astype(bf16)
        other = swap(kept, "fsdp", half >> b)
        if meanwhile is not None:
            other = after(other, *meanwhile(kept))
        order = [i ^ step for i in range(half)]
        total = kept.astype(f32) + jnp.stack([other[i] for i in order]).astype(f32)
    return total


def to_owner(partial):
    count = lax.axis_size("fsdp")
    held = partial
    mask = 1
    while held.shape[0] > 1:
        half = held.shape[0] // 2
        held = held[:half] + swap(held[half:].astype(bf16), "fsdp", mask).astype(f32)
        mask *= 2
    return held[0]


def gather_fsdp(value):
    held = value[None]
    mask = lax.axis_size("fsdp") // 2
    while mask:
        held = jnp.concatenate([held, swap(held, "fsdp", mask)], axis=0)
        mask //= 2
    return held


def reversed_bits(value, count):
    result = value * 0
    for b in range(bits_of(count)):
        result = result + ((value >> b) & 1) * (count >> (b + 1))
    return result


def on_device(
    inputs,
    block_order,
    cotangent,
    first_gain,
    first_shift,
    qkv_weight,
    qv_bias,
    proj_weight,
    proj_bias,
    second_gain,
    second_shift,
    fc_weight,
    fc_bias,
    down_weight,
    down_bias,
):
    nctx = lax.axis_size("ctx")
    nf = lax.axis_size("fsdp")
    c = lax.axis_index("ctx")
    f = lax.axis_index("fsdp")
    _, rows_dev, width = inputs.shape
    piece = width // nf
    heads = piece // HD
    ff = down_weight.shape[0]
    block_rows = rows_dev * nctx // block_order.shape[0]
    group = nctx // nf
    s, g = c // group, c % group
    scale = 1.0 / math.sqrt(HD)

    at = jnp.stack([f, s]).astype(jnp.int32)
    me = at[:1]
    own = inputs[0]
    tokens_b = [own]
    mask = nf // 2
    while mask:
        tokens_b = tokens_b + [swap(block, "fsdp", mask) for block in tokens_b]
        mask //= 2
    cut = kernel_call(cut_qkv_kernel, [((piece, 3 * piece), bf16)] * nf, (me,), (qkv_weight,))
    w_pieces = [swap(cut[k], "fsdp", k) if k else cut[k] for k in range(nf)]
    parts = [first_gain, first_shift, proj_bias, second_gain, second_shift, down_bias, qv_bias]
    parts = lax.optimization_barrier((*parts, cut[0]))[:-1]
    vectors = jnp.concatenate(parts).reshape(-1, 128)
    vectors_all = gather_fsdp(vectors).reshape(nf, 8, piece).astype(f32)
    owner_of = jnp.arange(nf, dtype=jnp.int32)
    slot_of = reversed_bits(owner_of ^ f, nf)
    pick = slot_of[:, None] == owner_of[None, :]
    in_order = jnp.sum(
        jnp.where(pick[:, :, None, None], vectors_all[None], 0.0), axis=1
    )
    flat = in_order[:, :6].transpose(1, 0, 2).reshape(6, width)
    gain1, shift1, pbias, gain2, shift2, dbias = (flat[i] for i in range(6))
    qv_flat = in_order[:, 6:].reshape(2, nf, piece)
    mine = (owner_of == f)[None, :, None]
    qv_mine = jnp.sum(jnp.where(mine, qv_flat, 0.0), axis=1)
    bias_row = jnp.concatenate([qv_mine[:1], jnp.zeros((1, piece), f32), qv_mine[1:]], axis=1)

    shape_q, shape_kv = ((piece, rows_dev), bf16), ((2 * piece, rows_dev), bf16)
    results = kernel_call(
        functools.partial(project_kernel, nf),
        [shape_q] * nf
        + [shape_kv] * nf
        + [
            ((nf, rows_dev, width), bf16),
            ((nf, rows_dev, width), f32),
            ((width, 3 * piece), bf16),
        ],
        (at,),
        [w_pieces[0], *tokens_b, flat[:1], flat[1:2], bias_row, *w_pieces[1:]],
        scratch=[pltpu.VMEM((nf, rows_dev, width), bf16)],
        cost=2 * nf * rows_dev * width * 3 * piece,
    )
    q_blocks, kv_blocks = results[:nf], results[nf : 2 * nf]
    hidden1, normed1, w_qkv = results[2 * nf :]
    upstream = gather_fsdp(after(cotangent[0], kv_blocks[0]))
    cut = kernel_call(
        cut_fc_kernel, [((piece, ff), bf16)] * nf, (me,), (after(fc_weight, kv_blocks[0]),)
    )
    cut = [swap(cut[k], "fsdp", k) if k else cut[k] for k in range(nf)]
    (w_fc,) = kernel_call(join_kernel, [((width, ff), bf16)], (me,), cut)
    tokens_half = jnp.stack(tokens_b[: nf // 2]).astype(f32)
    _, inverse1 = normalize(own.astype(f32))

    def across(blocks):
        return [swap(b, "ctx", j * group) if j else b for j, b in enumerate(blocks)]

    kv_all = across(kv_blocks)
    q_blocks = across(q_blocks)
    mask = group // 2
    while mask:
        kv_all = kv_all + [swap(block, "ctx", mask) for block in kv_all]
        mask //= 2
    members = reversed_bits(jnp.arange(group, dtype=jnp.int32), group) ^ g
    own_group = s ^ owner_of
    q_pos = positions_of(block_order, own_group * group + g, rows_dev, block_rows).reshape(1, -1)
    k_from = (own_group[None, :] * group + members[:, None]).reshape(-1)
    per_dev = rows_dev // block_rows
    stored = (k_from[:, None] * per_dev + jnp.arange(per_dev, dtype=jnp.int32)).reshape(-1)
    matches = stored[:, None] == jnp.arange(block_order.shape[0], dtype=jnp.int32)
    k_blocks = jnp.sum(jnp.where(matches, block_order, 0), axis=1)
    nq, nk = nf * rows_dev, nctx * rows_dev
    flops = 2 * heads * HD * nq * nk
    results = kernel_call(
        functools.partial(attend_kernel, nf, nctx, block_rows, heads),
        [((heads, nk, nq), bf16)] + [shape_q] * nf,
        (k_blocks,),
        [after(q_pos, w_fc, upstream), *q_blocks, *kv_all],
        scratch=[pltpu.VMEM((nk, nq), f32)],
        cost=2 * flops,
    )
    weights, att_out = results[0], results[1:]

    def collect(blocks):
        out = jnp.zeros((nf,) + blocks[0].shape, blocks[0].dtype)
        for j, block in enumerate(across(blocks)):
            out = lax.dynamic_update_index_in_dim(out, block, s ^ j, 0)
        return out

    att = collect(att_out)

    half = nf // 2
    total = sum_over_fsdp(dotf("pft,fo->pto", att, proj_weight))
    residual = tokens_half + total + pbias
    normed2, inverse2 = normalize(residual)
    hidden2_half = (normed2 * gain2 + shift2).astype(bf16)
    hidden2 = jnp.concatenate([hidden2_half, swap(hidden2_half, "fsdp", 1)], axis=0)
    rows_all = nf * rows_dev
    hidden2 = hidden2.reshape(rows_all, width)
    hidden_pre = dotf("te,eh->th", hidden2, w_fc) + fc_bias.astype(f32)
    activation, derivative = gelu_pair(hidden_pre)
    activation_b = activation.astype(bf16)
    up_rows = upstream.reshape(rows_all, width)
    pre_grad = dotf("to,ho->th", up_rows, down_weight) * derivative
    pre_grad_b = pre_grad.astype(bf16)
    second_part = dotf("th,eh->te", pre_grad_b, w_fc).reshape(nf, rows_dev, width)

    nbits, gbits, sbits = bits_of(nctx), bits_of(group), bits_of(nf)
    bit = [(c >> b) & 1 for b in range(nbits)]
    down_steps, fc_steps = [], []

    def start_gradients(point):
        rows = after(hidden2, point)
        held = dotf("te,th->eh", rows, pre_grad_b)
        for b in reversed(range(gbits)):
            w = held.shape[1] // 2
            held = (held[:, :w], held[:, w:])
            fc_steps.append((held, b))
            if b:
                held = finish(*begin(held, bit[b], 1 << b), 1 << b)
        held = dotf("to,th->oh", after(up_rows, point), activation_b)
        held = held.reshape((2,) * nbits + (width // nctx, ff))
        at = (slice(None),) * (nbits - 1)
        down_steps.append(((held[at + (0,)], held[at + (1,)]), 0))
        sends = []
        for steps in (fc_steps, down_steps):
            (halves, b) = steps[-1]
            keep, send = begin(halves, bit[b], 1 << b)
            steps.append((keep, send, b))
            sends.append(send)
        return sends

    second_grad = sum_over_fsdp(second_part, start_gradients)
    up_half = upstream[:half].astype(f32)
    residual_grad = up_half + norm_backward(second_grad, normed2, inverse2, gain2)
    rgrad_half = residual_grad.astype(bf16)
    rgrad = jnp.concatenate([rgrad_half, swap(rgrad_half, "fsdp", 1)], axis=0)
    agrad = dotf("fo,pto->pft", proj_weight, rgrad).astype(bf16)

    do_blocks = across(
        [lax.dynamic_index_in_dim(agrad, s ^ j, 0, keepdims=False) for j in range(nf)]
    )
    def lowest(value, b):
        at = (slice(None),) * (value.ndim - 3)
        return value[at + (0,)], value[at + (1,)]

    keep, send, b = fc_steps[-1]
    held = finish(keep, send, 1 << b, do_blocks[0])
    held = held.reshape((2,) * sbits + (piece, held.shape[1]))
    fc_keep, fc_send = begin(lowest(held, 0), bit[gbits], 1 << gbits)
    keep, send, b = down_steps[-1]
    held = finish(keep, send, 1 << b, do_blocks[0])
    down_keep, down_send = begin(lowest(held, 0), bit[1], 2)
    g_proj = dotf("pft,pto->fo", att, after(rgrad, do_blocks[0]))
    w = width // 2
    low, high = (0, nbits - 1)
    proj_keep, proj_send = begin((g_proj[:, :w], g_proj[:, w:]), bit[nbits - 1], nctx // 2)
    do_blocks[0] = after(do_blocks[0], fc_send, down_send, proj_send)
    results = kernel_call(
        functools.partial(attend_back_kernel, nf, nctx, heads),
        [shape_q] * nf + [(shape_kv[0], f32)] * nf + [shape_kv] * (nctx - nf),
        (),
        [weights, *q_blocks, *do_blocks, *att_out, *kv_all],
        cost=4 * flops,
    )
    dq_blocks, dkv = results[:nf], results[nf:]
    mask = 1
    while len(dkv) > nf:
        h = len(dkv) // 2
        came = [swap(block.astype(bf16), "ctx", mask) for block in dkv[h:]]
        dkv = [mine.astype(f32) + other.astype(f32) for mine, other in zip(dkv[:h], came)]
        mask *= 2
    dq_own = collect([after(block, came[0]) for block in dq_blocks])
    dkv_own = collect([block.astype(bf16) for block in dkv])
    qkv_grad = jnp.concatenate([dq_own, dkv_own], axis=1)

    g_qkv = dotf("pft,pte->fe", qkv_grad, hidden1)
    w = width // 2
    qkv_keep, qkv_send = begin((g_qkv[:, :w], g_qkv[:, w:]), bit[0], 1)
    qkv_grad = after(qkv_grad, qkv_send)
    first_part = dotf("pft,ef->pte", qkv_grad, w_qkv)
    first_grad = to_owner(first_part)
    input_grad = residual_grad[0] + norm_backward(first_grad, normed1[0], inverse1, gain1)

    late_point = qkv_send
    block_out = residual[0] + to_owner(
        dotf("th,ho->to", after(activation_b, late_point), down_weight).reshape(nf, rows_dev, width)
    ) + dbias

    device = c * nf + f
    held = finish(fc_keep, fc_send, 1 << gbits, late_point)
    for b in range(gbits + 1, nbits):
        held = halve(lowest(held, 0), bit[b], 1 << b)
    pairs = []
    for cc in range(nctx):
        for fi in range(nf):
            pairs.append((cc * nf + fi, (fi * group + cc % group) * nf + cc // group))
    g_fc = lax.ppermute(held.astype(bf16), ("ctx", "fsdp"), pairs).astype(f32)

    held = finish(down_keep, down_send, 2, late_point)
    for b in range(2, nbits):
        held = halve(lowest(held, 0), bit[b], 1 << b)
    g_down = held.T

    held = finish(proj_keep, proj_send, nctx // 2, late_point)
    for b in reversed(range(nbits - 1)):
        w = held.shape[1] // 2
        held = halve((held[:, :w], held[:, w:]), bit[b], 1 << b)
    g_proj = held

    held = finish(qkv_keep, qkv_send, 1)
    for b in range(1, sbits):
        w = held.shape[1] // 2
        held = halve((held[:, :w], held[:, w:]), bit[b], 1 << b)
    held = held.reshape((2,) * (nbits - sbits) + (-1, piece))
    for b in range(sbits, nbits):
        held = halve(lowest(held, 0), bit[b], 1 << b)
    unit = width // nctx
    units = held.astype(bf16).reshape(3, unit, piece)
    got = []
    for i in range(3):
        pairs = []
        for cc in range(nctx):
            r = sum(((cc >> b) & 1) * (nf >> (b + 1)) for b in range(sbits))
            for fi in range(nf):
                row = ((cc >> sbits) * 3 + (i - group * fi) % 3) * unit
                column = (row // piece) * width + fi * piece + row % piece
                assert (column // unit) % 3 == i
                pairs.append((cc * nf + fi, (column // (3 * unit)) * nf + r))
        which = (i + 3 * group * nf - group * f) % 3
        sent = lax.dynamic_index_in_dim(units, which, 0, keepdims=False)
        got.append(lax.ppermute(sent, ("ctx", "fsdp"), pairs))
    g_qkv_own = jnp.concatenate(got, axis=0).T.astype(f32)

    once = jnp.where(f < half, 1.0, 0.0)
    sums = [
        jnp.sum(up_half, axis=(0, 1)) * once,
        jnp.sum(residual_grad, axis=(0, 1)) * once,
        jnp.sum(second_grad * normed2, axis=(0, 1)) * once,
        jnp.sum(second_grad, axis=(0, 1)) * once,
        jnp.sum(first_part * normed1, axis=(0, 1)),
        jnp.sum(first_part, axis=(0, 1)),
        jnp.sum(pre_grad, axis=0),
        jnp.sum(qkv_grad[:, :piece].astype(f32), axis=(0, 2)),
        jnp.sum(qkv_grad[:, 2 * piece :].astype(f32), axis=(0, 2)),
    ]
    sums = jnp.concatenate(sums).reshape(-1, 128)
    for b in range(nbits):
        sums = sums + swap(sums, "ctx", 1 << b)
    shared = 6 * width // 128
    common, slices = sums[:shared], sums[None, shared:]
    mask = 1
    while mask < nf:
        came = swap(jnp.concatenate([common, slices.reshape(-1, 128)]), "fsdp", mask)
        common = common + came[:shared]
        slices = jnp.concatenate([slices, came[shared:].reshape(slices.shape)], axis=0)
        mask *= 2
    slices = slices.reshape(nf, -1)
    fc_sums, qv_sums = slices[:, :ff], slices[:, ff:]

    size = width // (nctx * nf)
    six = common.reshape(6, width)
    own = lax.dynamic_slice_in_dim(six, device * size, size, 1)
    start = device * 2 * size
    part, rest = start // width, start % width
    qv_own = lax.dynamic_slice_in_dim(
        qv_sums.reshape(-1),
        (((rest // piece) ^ f) * 2 + part) * piece + rest % piece,
        2 * size,
        0,
    )
    fsize = ff // nctx
    start = device * fsize
    fc_own = lax.dynamic_slice_in_dim(
        fc_sums.reshape(-1), ((start // ff) ^ f) * ff + start % ff, fsize, 0
    )
    return (
        block_out.astype(bf16)[None],
        input_grad[None],
        own[4],
        own[5],
        g_qkv_own,
        qv_own,
        g_proj,
        own[1],
        own[2],
        own[3],
        g_fc,
        fc_own,
        g_down,
        own[0],
    )


def solution(mesh):
    vector, matrix = P("fsdp"), P("fsdp", None)
    placed = (
        P("fsdp", "ctx", None),
        P(),
        P("fsdp", "ctx", None),
        vector,
        vector,
        matrix,
        vector,
        matrix,
        vector,
        vector,
        vector,
        matrix,
        vector,
        matrix,
        vector,
    )
    spread, block = P(("ctx", "fsdp")), P("fsdp", "ctx")
    return jax.shard_map(
        on_device,
        mesh=mesh,
        in_specs=placed,
        out_specs=(
            P("fsdp", "ctx", None),
            P("fsdp", "ctx", None),
            spread,
            spread,
            block,
            spread,
            block,
            spread,
            spread,
            spread,
            block,
            spread,
            block,
            spread,
        ),
        check_vma=False,
    )
```

```python
import functools
import math

import jax
import jax.numpy as jnp
from jax import lax
from jax.experimental import pallas as pl
from jax.experimental.pallas import tpu as pltpu
from jax.sharding import PartitionSpec as P


HD = 64

epsilon = 1e-05
negative_big = -1e30
gelu_coeff = 0.7978845608028654
bf16 = jnp.bfloat16
f32 = jnp.float32


def swap(value, axis, mask):
    count = lax.axis_size(axis)
    return lax.ppermute(value, axis, [(i, i ^ mask) for i in range(count)])


def bits_of(count):
    return count.bit_length() - 1


def normalize(rows):
    center = rows - jnp.mean(rows, axis=-1, keepdims=True)
    inverse = lax.rsqrt(jnp.mean(center * center, axis=-1, keepdims=True) + epsilon)
    return center * inverse, inverse


def norm_backward(grad_out, normed, inverse, gain):
    scaled = grad_out * gain
    return inverse * (
        scaled
        - jnp.mean(scaled, axis=-1, keepdims=True)
        - normed * jnp.mean(scaled * normed, axis=-1, keepdims=True)
    )


def gelu_pair(hidden_pre):
    argument = gelu_coeff * (hidden_pre + 0.044715 * hidden_pre * hidden_pre * hidden_pre)
    tangent = jnp.tanh(argument)
    result = 0.5 * hidden_pre * (1.0 + tangent)
    derivative = 0.5 * (1.0 + tangent) + 0.5 * hidden_pre * (
        1.0 - tangent * tangent
    ) * gelu_coeff * (1.0 + 3.0 * 0.044715 * hidden_pre * hidden_pre)
    return (result, derivative)


def dotf(spec, left, right):
    return jnp.einsum(spec, left, right, preferred_element_type=f32)


def positions_of(block_order, owners, rows_dev, block_rows):
    per_dev = rows_dev // block_rows
    row = jnp.arange(rows_dev, dtype=jnp.int32)
    stored = owners[:, None] * per_dev + (row // block_rows)[None, :]
    matches = stored[:, :, None] == jnp.arange(block_order.shape[0], dtype=jnp.int32)
    blocks = jnp.sum(jnp.where(matches, block_order, 0), axis=2)
    return blocks * block_rows + (row % block_rows)[None, :]


def after(value, *others):
    return lax.optimization_barrier((value,) + others)[0]


def whole(count):
    return [pl.BlockSpec(memory_space=pltpu.VMEM)] * count


def kernel_call(kernel, outs, scalars, operands, scratch=(), cost=0):
    smem = [pl.BlockSpec(memory_space=pltpu.SMEM)] * len(scalars)
    return pl.pallas_call(
        kernel,
        out_shape=[jax.ShapeDtypeStruct(shape, dtype) for shape, dtype in outs],
        in_specs=smem + whole(len(operands)),
        out_specs=whole(len(outs)),
        scratch_shapes=list(scratch),
        compiler_params=pltpu.CompilerParams(vmem_limit_bytes=60 * 1024 * 1024),
        cost_estimate=pl.CostEstimate(flops=cost, bytes_accessed=1 << 20, transcendentals=0),
    )(*scalars, *operands)


def contract(left, right, dims):
    return lax.dot_general(left, right, ((dims[0], dims[1]), ((), ())), preferred_element_type=f32)


def cut_qkv_kernel(me_ref, w_ref, *outs):
    count = len(outs)
    piece = outs[0].shape[1] // 3
    me = me_ref[0]
    for t in range(count):
        for k in range(count):

            @pl.when((me ^ k) == t)
            def _():
                for part in range(3):
                    start = (part * count + t) * piece
                    outs[k][:, part * piece : (part + 1) * piece] = w_ref[:, start : start + piece]


def cut_fc_kernel(me_ref, w_ref, *outs):
    ff = outs[0].shape[1]
    for k in range(len(outs)):
        start = pl.multiple_of((me_ref[0] ^ k) * ff, 128)
        outs[k][...] = w_ref[:, pl.ds(start, ff)]


def project_kernel(nf, at_ref, own_ref, *refs):
    x_refs, vec_refs = refs[:nf], refs[nf : 2 * nf]
    w_refs = (own_ref,) + refs[2 * nf : 3 * nf - 1]
    refs = refs[3 * nf - 1 :]
    q_refs, kv_refs = refs[:nf], refs[nf : 2 * nf]
    hidden_ref, normed_ref, inverse_ref, w_out, flat_ref, x_scr, vec_scr = refs[2 * nf :]
    me, group = at_ref[0], at_ref[1]
    piece = own_ref.shape[0]
    for k in range(nf):
        w_out[pl.ds(pl.multiple_of((me ^ k) * piece, piece), piece), :] = w_refs[k][...]
        x_scr[k] = x_refs[k][...]
        vec_scr[me ^ reversed_bits(k, nf)] = vec_refs[k][...].astype(f32)
    for k in range(nf):
        flat_ref[:, k * piece : (k + 1) * piece] = vec_scr[k]
    q_row = vec_scr[me // 2, pl.ds(6 + me % 2, 1), :]
    v_row = vec_scr[nf // 2 + me // 2, pl.ds(6 + me % 2, 1), :]
    bias = jnp.concatenate([q_row, jnp.zeros_like(q_row), v_row], axis=1)
    gain, shift = flat_ref[0:1, :], flat_ref[1:2, :]
    for j in range(nf):
        rows = x_scr[group ^ j].astype(f32)
        normed, inverse = normalize(rows)
        hidden = (normed * gain + shift).astype(bf16)
        normed_ref[group ^ j] = normed
        inverse_ref[group ^ j] = jnp.broadcast_to(inverse, (rows.shape[0], 128))
        hidden_ref[group ^ j] = hidden
        result = contract(hidden, w_out[...], ((1,), (0,))) + bias
        turned = result.T.astype(bf16)
        q_refs[j][...] = turned[:piece]
        kv_refs[j][...] = turned[piece:]


def feed_kernel(nf, me_ref, *refs):
    hid_refs, up_refs, w_refs = refs[:2], refs[2 : 2 + nf], refs[2 + nf : 2 + 2 * nf]
    down_ref, bias_ref = refs[2 + 2 * nf : 4 + 2 * nf]
    refs = refs[4 + 2 * nf :]
    hidden_ref, up_ref, act_ref, pre_ref, keep_ref, send_ref, sum_ref, w_scr = refs
    rows = up_refs[0].shape[0]
    piece = w_refs[0].shape[0]
    for k in range(nf):
        w_scr[pl.ds(pl.multiple_of((me_ref[0] ^ k) * piece, piece), piece), :] = w_refs[k][...]
    total = jnp.zeros(sum_ref.shape, f32)
    for p in range(nf):
        at = slice(p * rows, (p + 1) * rows)
        inner = (p * rows) % hid_refs[0].shape[0]
        hidden = hid_refs[2 * p // nf][inner : inner + rows, :]
        upper = up_refs[p][...]
        hidden_ref[at, :] = hidden
        up_ref[at, :] = upper
        pre = contract(hidden, w_scr[...], ((1,), (0,))) + bias_ref[...].astype(f32)
        activation, derivative = gelu_pair(pre)
        act_ref[at, :] = activation.astype(bf16)
        grad = contract(upper, down_ref[...], ((1,), (1,))) * derivative
        total = total + jnp.sum(grad, axis=0, keepdims=True)
        grad_b = grad.astype(bf16)
        pre_ref[at, :] = grad_b
        second = contract(grad_b, w_scr[...], ((1,), (1,)))
        if 2 * p < nf:
            keep_ref[at, :] = second
        else:
            send_ref[inner : inner + rows, :] = second.astype(bf16)
    sum_ref[...] = total


def turn_back_kernel(nf, group_ref, near_ref, far_ref, proj_ref, rgrad_ref, *refs):
    outs, scr = refs[:nf], refs[nf]
    for p in range(nf):
        rows = (near_ref if 2 * p < nf else far_ref)[p % (nf // 2)]
        rgrad_ref[p] = rows
        scr[p] = contract(proj_ref[...], rows, ((1,), (1,))).astype(bf16)
    for j in range(nf):
        outs[j][...] = scr[group_ref[0] ^ j]


def attend_kernel(nf, members, block_rows, heads, kb_ref, qpos_ref, *refs):
    q_refs, kv_refs = refs[:nf], refs[nf : nf + members]
    p_ref = refs[nf + members]
    o_refs = refs[nf + members + 1 : nf + members + 1 + nf]
    s_scr = refs[-1]
    rows = kv_refs[0].shape[1]
    qpos = qpos_ref[...]
    scale = 1.0 / math.sqrt(HD)

    def one_head(h, carry):
        at = pl.ds(pl.multiple_of(h * HD, HD), HD)
        at_v = pl.ds(pl.multiple_of((heads + h) * HD, HD), HD)
        q = jnp.concatenate([ref[at, :] for ref in q_refs], axis=1)
        largest = jnp.full((1, q.shape[1]), negative_big, f32)
        for i in range(members):
            scores = contract(kv_refs[i][at, :], q, ((0,), (0,))) * scale
            for b in range(rows // block_rows):
                part = scores[b * block_rows : (b + 1) * block_rows]
                pos = kb_ref[i * (rows // block_rows) + b] * block_rows
                pos = pos + lax.broadcasted_iota(jnp.int32, part.shape, 0)
                part = jnp.where(pos <= qpos, part, negative_big)
                start = i * rows + b * block_rows
                s_scr[start : start + block_rows, :] = part
                largest = jnp.maximum(largest, jnp.max(part, axis=0, keepdims=True))
        total = jnp.zeros_like(largest)
        for i in range(members):
            raised = jnp.exp(s_scr[i * rows : (i + 1) * rows, :] - largest)
            s_scr[i * rows : (i + 1) * rows, :] = raised
            total = total + jnp.sum(raised, axis=0, keepdims=True)
        inverse = 1.0 / total
        mixed = jnp.zeros((HD, q.shape[1]), f32)
        for i in range(members):
            weights = (s_scr[i * rows : (i + 1) * rows, :] * inverse).astype(bf16)
            p_ref[h, i * rows : (i + 1) * rows, :] = weights
            mixed = mixed + contract(kv_refs[i][at_v, :], weights, ((1,), (0,)))
        mixed = mixed.astype(bf16)
        for j in range(nf):
            o_refs[j][at, :] = mixed[:, j * rows : (j + 1) * rows]
        return carry

    lax.fori_loop(0, heads, one_head, 0)


def attend_back_kernel(nf, members, heads, p_ref, *refs):
    q_refs, do_refs, o_refs = refs[:nf], refs[nf : 2 * nf], refs[2 * nf : 3 * nf]
    kv_refs = refs[3 * nf : 3 * nf + members]
    dq_refs = refs[3 * nf + members : 4 * nf + members]
    dkv_refs = refs[4 * nf + members :]
    rows = kv_refs[0].shape[1]
    scale = 1.0 / math.sqrt(HD)

    def one_head(h, carry):
        at = pl.ds(pl.multiple_of(h * HD, HD), HD)
        at_v = pl.ds(pl.multiple_of((heads + h) * HD, HD), HD)
        q = jnp.concatenate([ref[at, :] for ref in q_refs], axis=1)
        do = jnp.concatenate([ref[at, :] for ref in do_refs], axis=1)
        o = jnp.concatenate([ref[at, :] for ref in o_refs], axis=1)
        delta = jnp.sum(do.astype(f32) * o.astype(f32), axis=0, keepdims=True)
        dq = jnp.zeros(q.shape, f32)
        for i in range(members):
            weights = p_ref[h, i * rows : (i + 1) * rows, :]
            prob_grad = contract(kv_refs[i][at_v, :], do, ((0,), (0,)))
            score_grad = (weights.astype(f32) * (prob_grad - delta)).astype(bf16)
            kind = dkv_refs[i].dtype
            dkv_refs[i][at_v, :] = contract(do, weights, ((1,), (1,))).astype(kind)
            dkv_refs[i][at, :] = (contract(q, score_grad, ((1,), (1,))) * scale).astype(kind)
            dq = dq + contract(kv_refs[i][at, :], score_grad, ((1,), (0,)))
        dq = (dq * scale).astype(bf16)
        for j in range(nf):
            dq_refs[j][at, :] = dq[:, j * rows : (j + 1) * rows]
        return carry

    lax.fori_loop(0, heads, one_head, 0)


def begin(halves, bit):
    low, high = halves
    return jnp.where(bit == 0, low, high), jnp.where(bit == 0, high, low).astype(bf16)


def sum_over_fsdp(kept, sent, meanwhile=None):
    count = lax.axis_size("fsdp")
    half = count // 2
    total = kept + swap(sent, "fsdp", 1).astype(f32)
    for b in range(bits_of(half)):
        step = 1 << b
        kept = total.astype(bf16)
        other = swap(kept, "fsdp", half >> b)
        if meanwhile is not None:
            other = after(other, *meanwhile(kept))
        order = [i ^ step for i in range(half)]
        total = kept.astype(f32) + jnp.stack([other[i] for i in order]).astype(f32)
    return total


def to_owner(partial):
    held = partial
    mask = 1
    while held.shape[0] > 1:
        half = held.shape[0] // 2
        held = held[:half] + swap(held[half:].astype(bf16), "fsdp", mask).astype(f32)
        mask *= 2
    return held[0]


def reversed_bits(value, count):
    result = value * 0
    for b in range(bits_of(count)):
        result = result + ((value >> b) & 1) * (count >> (b + 1))
    return result


def on_device(
    inputs,
    block_order,
    cotangent,
    first_gain,
    first_shift,
    qkv_weight,
    qv_bias,
    proj_weight,
    proj_bias,
    second_gain,
    second_shift,
    fc_weight,
    fc_bias,
    down_weight,
    down_bias,
):
    nctx = lax.axis_size("ctx")
    nf = lax.axis_size("fsdp")
    c = lax.axis_index("ctx")
    f = lax.axis_index("fsdp")
    _, rows_dev, width = inputs.shape
    piece = width // nf
    heads = piece // HD
    ff = down_weight.shape[0]
    block_rows = rows_dev * nctx // block_order.shape[0]
    group = nctx // nf
    s, g = c // group, c % group
    half = nf // 2

    at = jnp.stack([f, s]).astype(jnp.int32)
    me = at[:1]
    own = inputs[0]
    tokens_b = [own]
    mask = nf // 2
    while mask:
        tokens_b = tokens_b + [swap(block, "fsdp", mask) for block in tokens_b]
        mask //= 2
    cut = kernel_call(cut_qkv_kernel, [((piece, 3 * piece), bf16)] * nf, (me,), (qkv_weight,))
    w_pieces = [swap(cut[k], "fsdp", k) if k else cut[k] for k in range(nf)]
    parts = [first_gain, first_shift, proj_bias, second_gain, second_shift, down_bias, qv_bias]
    parts = lax.optimization_barrier((*parts, tokens_b[1]))[:-1]
    vectors_all = [jnp.concatenate(parts).reshape(8, piece)]
    mask = nf // 2
    while mask:
        vectors_all = vectors_all + [swap(block, "fsdp", mask) for block in vectors_all]
        mask //= 2
    cut_fc = kernel_call(cut_fc_kernel, [((piece, ff), bf16)] * nf, (me,), (fc_weight,))

    shape_q, shape_kv = ((piece, rows_dev), bf16), ((2 * piece, rows_dev), bf16)
    results = kernel_call(
        functools.partial(project_kernel, nf),
        [shape_q] * nf
        + [shape_kv] * nf
        + [
            ((nf, rows_dev, width), bf16),
            ((nf, rows_dev, width), f32),
            ((nf, rows_dev, 128), f32),
            ((width, 3 * piece), bf16),
            ((8, width), f32),
        ],
        (at,),
        [after(w_pieces[0], cut_fc[0]), *tokens_b, *vectors_all, *w_pieces[1:]],
        scratch=[
            pltpu.VMEM((nf, rows_dev, width), bf16),
            pltpu.VMEM((nf, 8, piece), f32),
        ],
        cost=2 * nf * rows_dev * width * 3 * piece,
    )
    q_blocks, kv_blocks = results[:nf], results[nf : 2 * nf]
    hidden1, normed1, inverse1, w_qkv, flat = results[2 * nf :]
    pbias, gain2, shift2, dbias = (flat[i : i + 1] for i in range(2, 6))
    gain1 = flat[:1]
    tokens_half = jnp.stack(tokens_b[: nf // 2])

    def across(blocks):
        return [swap(b, "ctx", j * group) if j else b for j, b in enumerate(blocks)]

    kv_all = across(kv_blocks)
    q_blocks = across(q_blocks)
    upstream = [after(cotangent[0], kv_all[1])]
    mask = half
    while mask:
        upstream = upstream + [swap(block, "fsdp", mask) for block in upstream]
        mask //= 2
    fc_pieces = [
        swap(after(cut_fc[k], kv_all[1]), "fsdp", k) if k else cut_fc[k] for k in range(nf)
    ]
    mask = group // 2
    while mask:
        kv_all = kv_all + [swap(block, "ctx", mask) for block in kv_all]
        mask //= 2
    members = reversed_bits(jnp.arange(group, dtype=jnp.int32), group) ^ g
    own_group = s ^ jnp.arange(nf, dtype=jnp.int32)
    q_pos = positions_of(block_order, own_group * group + g, rows_dev, block_rows).reshape(1, -1)
    k_from = (own_group[None, :] * group + members[:, None]).reshape(-1)
    per_dev = rows_dev // block_rows
    stored = (k_from[:, None] * per_dev + jnp.arange(per_dev, dtype=jnp.int32)).reshape(-1)
    matches = stored[:, None] == jnp.arange(block_order.shape[0], dtype=jnp.int32)
    k_blocks = jnp.sum(jnp.where(matches, block_order, 0), axis=1)
    nq, nk = nf * rows_dev, nctx * rows_dev
    flops = 2 * heads * HD * nq * nk
    results = kernel_call(
        functools.partial(attend_kernel, nf, nctx, block_rows, heads),
        [((heads, nk, nq), bf16)] + [shape_q] * nf,
        (k_blocks,),
        [q_pos, *q_blocks, *kv_all],
        scratch=[pltpu.VMEM((nk, nq), f32)],
        cost=2 * flops,
    )
    weights, att_out = results[0], results[1:]

    def collect(blocks, *points):
        out = jnp.zeros((nf,) + blocks[0].shape, blocks[0].dtype)
        for j, block in enumerate(across(blocks)):
            if points:
                block = after(block, *points)
            out = lax.dynamic_update_index_in_dim(out, block, s ^ j, 0)
        return out

    att = collect(att_out)

    part = dotf("pft,fo->pto", after(att, *fc_pieces, *upstream), proj_weight)
    total = sum_over_fsdp(part[:half], part[half:].astype(bf16))
    residual = tokens_half.astype(f32) + total + pbias
    normed2, inverse2 = normalize(residual)
    hidden2_half = (normed2 * gain2 + shift2).astype(bf16)
    rows_all = nf * rows_dev
    hidden2_half = hidden2_half.reshape(rows_all // 2, width)
    flops = 6 * rows_all * width * ff
    hidden2, up_rows, activation_b, pre_grad_b, second_keep, second_send, fc_sum = kernel_call(
        functools.partial(feed_kernel, nf),
        [
            ((rows_all, width), bf16),
            ((rows_all, width), bf16),
            ((rows_all, ff), bf16),
            ((rows_all, ff), bf16),
            ((rows_all // 2, width), f32),
            ((rows_all // 2, width), bf16),
            ((1, ff), f32),
        ],
        (me,),
        [hidden2_half, swap(hidden2_half, "fsdp", 1), *upstream, *fc_pieces]
        + [down_weight, fc_bias.reshape(1, ff)],
        scratch=[pltpu.VMEM((width, ff), bf16)],
        cost=flops,
    )

    nbits, gbits, sbits = bits_of(nctx), bits_of(group), bits_of(nf)
    bit = [(c >> b) & 1 for b in range(nbits)]
    state = {}

    def columns(value):
        w = value.shape[1] // 2
        return value[:, :w], value[:, w:]

    def step(name, halves, b):
        keep, send = begin(halves, bit[b])
        state[name] = (keep, send, swap(send, "ctx", 1 << b))
        return send

    def result_of(name, point=None):
        keep, _, came = state[name]
        if point is not None:
            came = after(came, point)
        return keep + came.astype(f32)

    down_order = [gbits] + [b for b in range(nbits) if b != gbits]

    def down_halves(value, b):
        left = down_order[down_order.index(b) :]
        axis = sum(1 for other in left if other > b)
        return lax.index_in_dim(value, 0, axis, False), lax.index_in_dim(value, 1, axis, False)

    def start_gradients(point):
        held = dotf("te,th->eh", after(hidden2, point), pre_grad_b)
        for b in reversed(range(gbits)):
            sent_fc = step("fc", columns(held), b)
            if b:
                held = result_of("fc")
        held = dotf("to,th->oh", after(up_rows, point), activation_b)
        held = held.reshape((2,) * nbits + (width // nctx, ff))
        sent_down = step("down", down_halves(held, down_order[0]), down_order[0])
        return sent_fc, sent_down

    second_keep = second_keep.reshape(half, rows_dev, width)
    second_send = second_send.reshape(half, rows_dev, width)
    second_grad = sum_over_fsdp(second_keep, second_send, start_gradients)
    up_half = up_rows[: rows_all // 2].reshape(half, rows_dev, width).astype(f32)
    residual_grad = up_half + norm_backward(second_grad, normed2, inverse2, gain2)
    rgrad_half = residual_grad.astype(bf16)
    rgrad_far = swap(rgrad_half, "fsdp", 1)
    rgrad, *do_blocks = kernel_call(
        functools.partial(turn_back_kernel, nf),
        [((nf, rows_dev, width), bf16)] + [shape_q] * nf,
        (at[1:],),
        [rgrad_half, rgrad_far, proj_weight],
        scratch=[pltpu.VMEM((nf, piece, rows_dev), bf16)],
        cost=2 * nf * rows_dev * width * piece,
    )

    do_blocks = across(do_blocks)

    def lowest(value):
        at = (slice(None),) * (value.ndim - 3)
        return value[at + (0,)], value[at + (1,)]

    held = result_of("fc", do_blocks[1])
    held = held.reshape((2,) * sbits + (piece, held.shape[1]))
    sent_fc = step("fc", lowest(held), gbits)
    held = result_of("down", do_blocks[1])
    sent_down = step("down", down_halves(held, down_order[1]), down_order[1])
    do_blocks[0] = after(do_blocks[0], sent_fc, sent_down)
    results = kernel_call(
        functools.partial(attend_back_kernel, nf, nctx, heads),
        [shape_q] * nf + [(shape_kv[0], f32)] * nf + [shape_kv] * (nctx - nf),
        (),
        [weights, *q_blocks, *do_blocks, *att_out, *kv_all],
        cost=10 * heads * HD * nq * nk,
    )
    dq_blocks, dkv = results[:nf], results[nf:]
    dq_blocks = list(lax.optimization_barrier(tuple(dq_blocks)))
    mask = 1
    while len(dkv) > nf:
        h = len(dkv) // 2
        came = [swap(block.astype(bf16), "ctx", mask) for block in dkv[h:]]
        dkv = [mine.astype(f32) + other.astype(f32) for mine, other in zip(dkv[:h], came)]
        mask *= 2
    dkv_sent = [block.astype(bf16) for block in dkv]
    dq_own = collect(dq_blocks, *dkv_sent)
    dkv_own = collect(dkv_sent)
    block_out = residual[0] + to_owner(
        dotf("th,ho->to", after(activation_b, *dkv_sent), down_weight).reshape(nf, rows_dev, width)
    ) + dbias
    g_proj = dotf("pft,pto->fo", att, after(rgrad, *dkv_sent))
    step("proj", columns(g_proj), nbits - 1)
    qkv_grad = jnp.concatenate([dq_own, dkv_own], axis=1)

    device = c * nf + f
    sent = step("qkv", columns(dotf("pft,pte->fe", qkv_grad, hidden1)), 0)
    ends = {}
    fc_b, down_b = gbits + 1, 2
    while fc_b < nbits or down_b < nbits:
        if fc_b < nbits:
            ends["fc"] = step("fc", lowest(result_of("fc", sent)), fc_b)
            fc_b += 1
        if down_b < nbits:
            b = down_order[down_b]
            ends["down"] = step("down", down_halves(result_of("down", sent), b), b)
            down_b += 1

    qkv_grad = after(qkv_grad, sent, *ends.values())
    first_part = dotf("pft,ef->pte", qkv_grad, w_qkv)
    first_grad = to_owner(first_part)
    input_grad = residual_grad[0] + norm_backward(
        first_grad, normed1[0], after(inverse1, sent)[0, :, :1], gain1
    )
    up_late, fc_sum = lax.optimization_barrier((up_rows, fc_sum, *dkv_sent))[:2]
    sums = [
        jnp.sum(up_late[: rows_all // 2].astype(f32), axis=0),
        jnp.sum(residual_grad, axis=(0, 1)),
        jnp.sum(second_grad * normed2, axis=(0, 1)),
        jnp.sum(second_grad, axis=(0, 1)),
        jnp.sum(first_part * normed1, axis=(0, 1)),
        jnp.sum(first_part, axis=(0, 1)),
        fc_sum.reshape(-1),
        jnp.sum(qkv_grad[:, :piece].astype(f32), axis=(0, 2)),
        jnp.sum(qkv_grad[:, 2 * piece :].astype(f32), axis=(0, 2)),
    ]
    sums = jnp.concatenate(sums).reshape(-1, 128)
    held_twice = jnp.arange(sums.shape[0])[:, None] < 4 * width // 128
    sums = jnp.where(held_twice & (f >= half), 0.0, sums)

    def next_sums(b, *points):
        came = swap(sums, "ctx", 1 << b)
        return sums + (after(came, *points) if points else came)


    held = result_of("qkv")
    for b in range(1, sbits):
        sent = step("qkv", columns(held), b)
        sums = next_sums(b - 1, sent)
        step("proj", columns(result_of("proj", sent)), nbits - 1 - b)
        held = result_of("qkv")
    held = held.reshape((2,) * (nbits - sbits) + (-1, piece))
    for b in range(sbits, nbits):
        sent = step("qkv", lowest(held), b)
        sums = next_sums(b - 1, sent)
        step("proj", columns(result_of("proj", sent)), nbits - 1 - b)
        held = result_of("qkv")
    g_proj = result_of("proj")
    g_down = result_of("down", sent).T
    last = result_of("fc", sent).astype(bf16)
    pairs = []
    for cc in range(nctx):
        for fi in range(nf):
            pairs.append((cc * nf + fi, (fi * group + cc % group) * nf + cc // group))
    g_fc = lax.ppermute(last, ("ctx", "fsdp"), pairs).astype(f32)
    unit = width // nctx
    units = held.astype(bf16).reshape(3, unit, piece)
    got = []
    for i in range(3):
        pairs = []
        for cc in range(nctx):
            r = sum(((cc >> b) & 1) * (nf >> (b + 1)) for b in range(sbits))
            for fi in range(nf):
                row = ((cc >> sbits) * 3 + (i - group * fi) % 3) * unit
                column = (row // piece) * width + fi * piece + row % piece
                assert (column // unit) % 3 == i
                pairs.append((cc * nf + fi, (column // (3 * unit)) * nf + r))
        which = (i + 3 * group * nf - group * f) % 3
        sent = lax.dynamic_index_in_dim(units, which, 0, keepdims=False)
        got.append(lax.ppermute(sent, ("ctx", "fsdp"), pairs))
    g_qkv_own = jnp.concatenate(got, axis=0).T.astype(f32)

    sums = next_sums(nbits - 1, units)
    shared = 6 * width // 128
    pieces = [sums]
    mask = nf // 2
    while mask:
        pieces = pieces + [swap(block, "fsdp", mask) for block in pieces]
        mask //= 2
    six = sum(block[:shared] for block in pieces).reshape(6, width)

    def slice_of(index, first, last):
        chosen = jnp.zeros((last - first, 128), f32)
        for k, block in enumerate(pieces):
            is_it = (index ^ f) == reversed_bits(k, nf)
            chosen = jnp.where(is_it, block[first:last], chosen)
        return chosen.reshape(-1)

    size = width // (nctx * nf)
    own = lax.dynamic_slice_in_dim(six, device * size, size, 1)
    start = device * 2 * size
    part, rest = start // width, start % width
    ends = shared + ff // 128
    qv_own = lax.dynamic_slice_in_dim(
        slice_of(rest // piece, ends, sums.shape[0]), part * piece + rest % piece, 2 * size, 0
    )
    fsize = ff // nctx
    start = device * fsize
    fc_own = lax.dynamic_slice_in_dim(slice_of(start // ff, shared, ends), start % ff, fsize, 0)
    return (
        block_out.astype(bf16)[None],
        input_grad[None],
        own[4],
        own[5],
        g_qkv_own,
        qv_own,
        g_proj,
        own[1],
        own[2],
        own[3],
        g_fc,
        fc_own,
        g_down,
        own[0],
    )


def solution(mesh):
    vector, matrix = P("fsdp"), P("fsdp", None)
    placed = (
        P("fsdp", "ctx", None),
        P(),
        P("fsdp", "ctx", None),
        vector,
        vector,
        matrix,
        vector,
        matrix,
        vector,
        vector,
        vector,
        matrix,
        vector,
        matrix,
        vector,
    )
    spread, block = P(("ctx", "fsdp")), P("fsdp", "ctx")

    return jax.shard_map(
        on_device,
        mesh=mesh,
        in_specs=placed,
        out_specs=(
            P("fsdp", "ctx", None),
            P("fsdp", "ctx", None),
            spread,
            spread,
            block,
            spread,
            block,
            spread,
            spread,
            spread,
            block,
            spread,
            block,
            spread,
        ),
        check_vma=False,
    )
```

```python
import functools
import math

import jax
import jax.numpy as jnp
from jax import lax
from jax.experimental import pallas as pl
from jax.experimental.pallas import tpu as pltpu
from jax.sharding import PartitionSpec as P


HD = 64

epsilon = 1e-05
negative_big = -1e30
gelu_coeff = 0.7978845608028654
bf16 = jnp.bfloat16
f32 = jnp.float32


def swap(value, axis, mask):
    count = lax.axis_size(axis)
    return lax.ppermute(value, axis, [(i, i ^ mask) for i in range(count)])


def bits_of(count):
    return count.bit_length() - 1


def normalize(rows):
    center = rows - jnp.mean(rows, axis=-1, keepdims=True)
    inverse = lax.rsqrt(jnp.mean(center * center, axis=-1, keepdims=True) + epsilon)
    return center * inverse, inverse


def norm_backward(grad_out, normed, inverse, gain):
    scaled = grad_out * gain
    return inverse * (
        scaled
        - jnp.mean(scaled, axis=-1, keepdims=True)
        - normed * jnp.mean(scaled * normed, axis=-1, keepdims=True)
    )


def gelu_pair(hidden_pre):
    argument = gelu_coeff * (hidden_pre + 0.044715 * hidden_pre * hidden_pre * hidden_pre)
    tangent = jnp.tanh(argument)
    result = 0.5 * hidden_pre * (1.0 + tangent)
    derivative = 0.5 * (1.0 + tangent) + 0.5 * hidden_pre * (
        1.0 - tangent * tangent
    ) * gelu_coeff * (1.0 + 3.0 * 0.044715 * hidden_pre * hidden_pre)
    return (result, derivative)


def dotf(spec, left, right):
    return jnp.einsum(spec, left, right, preferred_element_type=f32)


def positions_of(block_order, owners, rows_dev, block_rows):
    per_dev = rows_dev // block_rows
    row = jnp.arange(rows_dev, dtype=jnp.int32)
    stored = owners[:, None] * per_dev + (row // block_rows)[None, :]
    matches = stored[:, :, None] == jnp.arange(block_order.shape[0], dtype=jnp.int32)
    blocks = jnp.sum(jnp.where(matches, block_order, 0), axis=2)
    return blocks * block_rows + (row % block_rows)[None, :]


def after(value, *others):
    return lax.optimization_barrier((value,) + others)[0]


def whole(count):
    return [pl.BlockSpec(memory_space=pltpu.VMEM)] * count


def kernel_call(kernel, outs, scalars, operands, scratch=(), cost=0, grid=(), blocks=None):
    blocks = blocks or {}
    specs = whole(len(operands) + len(outs))
    for place, spec in blocks.items():
        specs[place] = spec
    smem = [pl.BlockSpec(memory_space=pltpu.SMEM)] * len(scalars)
    return pl.pallas_call(
        kernel,
        out_shape=[jax.ShapeDtypeStruct(shape, dtype) for shape, dtype in outs],
        grid=grid,
        in_specs=smem + specs[: len(operands)],
        out_specs=specs[len(operands) :],
        scratch_shapes=list(scratch),
        compiler_params=pltpu.CompilerParams(vmem_limit_bytes=60 * 1024 * 1024),
        cost_estimate=pl.CostEstimate(flops=cost, bytes_accessed=1 << 20, transcendentals=0),
    )(*scalars, *operands)


def contract(left, right, dims):
    return lax.dot_general(left, right, ((dims[0], dims[1]), ((), ())), preferred_element_type=f32)


def cut_qkv_kernel(me_ref, w_ref, *outs):
    count = len(outs)
    piece = outs[0].shape[1] // 3
    me = me_ref[0]
    for t in range(count):
        for k in range(count):

            @pl.when((me ^ k) == t)
            def _():
                for part in range(3):
                    start = (part * count + t) * piece
                    outs[k][:, part * piece : (part + 1) * piece] = w_ref[:, start : start + piece]


def cut_fc_kernel(me_ref, w_ref, *outs):
    ff = outs[0].shape[1]
    for k in range(len(outs)):
        start = pl.multiple_of((me_ref[0] ^ k) * ff, 128)
        outs[k][...] = w_ref[:, pl.ds(start, ff)]


def project_kernel(nf, at_ref, own_ref, *refs):
    x_refs, vec_refs = refs[:nf], refs[nf : 2 * nf]
    w_refs = (own_ref,) + refs[2 * nf : 3 * nf - 1]
    refs = refs[3 * nf - 1 :]
    q_refs, kv_refs = refs[:nf], refs[nf : 2 * nf]
    hidden_ref, normed_ref, inverse_ref, w_out, flat_ref = refs[2 * nf : 2 * nf + 5]
    x_scr, vec_scr, turn_scr = refs[2 * nf + 5 :]
    me, group = at_ref[0], at_ref[1]
    piece = own_ref.shape[0]
    for k in range(nf):
        w_out[pl.ds(pl.multiple_of((me ^ k) * piece, piece), piece), :] = w_refs[k][...]
        x_scr[k] = x_refs[k][...]
        vec_scr[me ^ reversed_bits(k, nf)] = vec_refs[k][...].astype(f32)
    for k in range(nf):
        flat_ref[:, k * piece : (k + 1) * piece] = vec_scr[k]
    q_row = vec_scr[me // 2, pl.ds(6 + me % 2, 1), :]
    v_row = vec_scr[nf // 2 + me // 2, pl.ds(6 + me % 2, 1), :]
    bias = jnp.concatenate([q_row, jnp.zeros_like(q_row), v_row], axis=1)
    gain, shift = flat_ref[0:1, :], flat_ref[1:2, :]
    count = x_scr.shape[1]
    for p in range(nf):
        normed, inverse = normalize(x_scr[p].astype(f32))
        normed_ref[p] = normed
        inverse_ref[p] = jnp.broadcast_to(inverse, (count, 128))
        hidden_ref[p] = (normed * gain + shift).astype(bf16)
    hidden = hidden_ref[...].reshape(nf * count, hidden_ref.shape[2])
    result = contract(hidden, w_out[...], ((1,), (0,))) + bias
    for p in range(nf):
        turn_scr[p] = result[p * count : (p + 1) * count].T.astype(bf16)
    for j in range(nf):
        turned = turn_scr[group ^ j]
        q_refs[j][...] = turned[:piece]
        kv_refs[j][...] = turned[piece:]


def feed_kernel(nf, me_ref, *refs):
    hid_refs, up_refs, w_refs = refs[:2], refs[2 : 2 + nf], refs[2 + nf : 2 + 2 * nf]
    down_ref, bias_ref = refs[2 + 2 * nf : 4 + 2 * nf]
    refs = refs[4 + 2 * nf :]
    hidden_ref, up_ref, act_ref, pre_ref, keep_ref, send_ref, sum_ref, w_scr = refs
    rows = up_refs[0].shape[0]
    piece = w_refs[0].shape[0]
    for k in range(nf):
        w_scr[pl.ds(pl.multiple_of((me_ref[0] ^ k) * piece, piece), piece), :] = w_refs[k][...]
    count = hid_refs[0].shape[0]
    for p in range(nf):
        up_ref[p * rows : (p + 1) * rows, :] = up_refs[p][...]
    hidden_ref[:count, :] = hid_refs[0][...]
    hidden_ref[count:, :] = hid_refs[1][...]
    pre = contract(hidden_ref[...], w_scr[...], ((1,), (0,))) + bias_ref[...].astype(f32)
    activation, derivative = gelu_pair(pre)
    act_ref[...] = activation.astype(bf16)
    grad = contract(up_ref[...], down_ref[...], ((1,), (1,))) * derivative
    sum_ref[...] = jnp.sum(grad, axis=0, keepdims=True)
    pre_ref[...] = grad.astype(bf16)
    second = contract(pre_ref[...], w_scr[...], ((1,), (1,)))
    keep_ref[...] = second[:count]
    send_ref[...] = second[count:].astype(bf16)


def turn_back_kernel(nf, group_ref, near_ref, far_ref, proj_ref, rgrad_ref, *refs):
    outs, scr = refs[:nf], refs[nf]
    half, count, width = near_ref.shape
    for n, ref in enumerate((near_ref, far_ref)):
        rows = ref[...]
        rgrad_ref[n * half : (n + 1) * half] = rows
        rows = rows.reshape(half * count, width)
        turned = contract(proj_ref[...], rows, ((1,), (1,))).astype(bf16)
        for p in range(half):
            scr[n * half + p] = turned[:, p * count : (p + 1) * count]
    for j in range(nf):
        outs[j][...] = scr[group_ref[0] ^ j]


def attend_kernel(nf, members, block_rows, heads, kb_ref, qpos_ref, *refs):
    q_refs, kv_refs = refs[:nf], refs[nf : nf + members]
    p_ref = refs[nf + members]
    o_refs = refs[nf + members + 1 : nf + members + 1 + nf]
    s_scr = refs[-1]
    rows = kv_refs[0].shape[1]
    qpos = qpos_ref[...]
    scale = 1.0 / math.sqrt(HD)

    def one_head(h):
        at = pl.ds(pl.multiple_of(h * HD, HD), HD)
        at_v = pl.ds(pl.multiple_of((heads + h) * HD, HD), HD)
        q = jnp.concatenate([ref[at, :] for ref in q_refs], axis=1)
        largest = jnp.full((1, q.shape[1]), negative_big, f32)
        for i in range(0, members, 2):
            keys = jnp.concatenate([kv_refs[i][at, :], kv_refs[i + 1][at, :]], axis=1)
            scores = contract(keys, q, ((0,), (0,))) * scale
            for b in range(2 * rows // block_rows):
                part = scores[b * block_rows : (b + 1) * block_rows]
                pos = kb_ref[i * (rows // block_rows) + b] * block_rows
                pos = pos + lax.broadcasted_iota(jnp.int32, part.shape, 0)
                part = jnp.where(pos <= qpos, part, negative_big)
                start = i * rows + b * block_rows
                s_scr[start : start + block_rows, :] = part
                largest = jnp.maximum(largest, jnp.max(part, axis=0, keepdims=True))
        total = jnp.zeros_like(largest)
        for i in range(members):
            raised = jnp.exp(s_scr[i * rows : (i + 1) * rows, :] - largest)
            s_scr[i * rows : (i + 1) * rows, :] = raised
            total = total + jnp.sum(raised, axis=0, keepdims=True)
        inverse = 1.0 / total
        mixed = jnp.zeros((HD, q.shape[1]), f32)
        for i in range(0, members, 2):
            weights = (s_scr[i * rows : (i + 2) * rows, :] * inverse).astype(bf16)
            p_ref[0, i * rows : (i + 2) * rows, :] = weights
            values = jnp.concatenate([kv_refs[i][at_v, :], kv_refs[i + 1][at_v, :]], axis=1)
            mixed = mixed + contract(values, weights, ((1,), (0,)))
        mixed = mixed.astype(bf16)
        for j in range(nf):
            o_refs[j][at, :] = mixed[:, j * rows : (j + 1) * rows]

    one_head(pl.program_id(0))


def attend_back_kernel(nf, members, heads, p_ref, *refs):
    q_refs, do_refs, o_refs = refs[:nf], refs[nf : 2 * nf], refs[2 * nf : 3 * nf]
    kv_refs = refs[3 * nf : 3 * nf + members]
    dq_refs = refs[3 * nf + members : 4 * nf + members]
    dkv_refs = refs[4 * nf + members :]
    rows = kv_refs[0].shape[1]
    scale = 1.0 / math.sqrt(HD)

    def one_head(h):
        at = pl.ds(pl.multiple_of(h * HD, HD), HD)
        at_v = pl.ds(pl.multiple_of((heads + h) * HD, HD), HD)
        q = jnp.concatenate([ref[at, :] for ref in q_refs], axis=1)
        do = jnp.concatenate([ref[at, :] for ref in do_refs], axis=1)
        o = jnp.concatenate([ref[at, :] for ref in o_refs], axis=1)
        delta = jnp.sum(do.astype(f32) * o.astype(f32), axis=0, keepdims=True)
        dq = jnp.zeros(q.shape, f32)
        for i in range(0, members, 2):
            weights = p_ref[0, i * rows : (i + 2) * rows, :]
            keys = jnp.concatenate([kv_refs[i][at, :], kv_refs[i + 1][at, :]], axis=1)
            values = jnp.concatenate([kv_refs[i][at_v, :], kv_refs[i + 1][at_v, :]], axis=1)
            prob_grad = contract(values, do, ((0,), (0,)))
            score_grad = (weights.astype(f32) * (prob_grad - delta)).astype(bf16)
            dv = contract(do, weights, ((1,), (1,)))
            dk = contract(q, score_grad, ((1,), (1,))) * scale
            for n in range(2):
                kind = dkv_refs[i + n].dtype
                dkv_refs[i + n][at_v, :] = dv[:, n * rows : (n + 1) * rows].astype(kind)
                dkv_refs[i + n][at, :] = dk[:, n * rows : (n + 1) * rows].astype(kind)
            dq = dq + contract(keys, score_grad, ((1,), (0,)))
        dq = (dq * scale).astype(bf16)
        for j in range(nf):
            dq_refs[j][at, :] = dq[:, j * rows : (j + 1) * rows]

    one_head(pl.program_id(0))


def begin(halves, bit):
    low, high = halves
    return jnp.where(bit == 0, low, high), jnp.where(bit == 0, high, low).astype(bf16)


def sum_over_fsdp(kept, sent, meanwhile=None):
    count = lax.axis_size("fsdp")
    half = count // 2
    total = kept + swap(sent, "fsdp", 1).astype(f32)
    for b in range(bits_of(half)):
        step = 1 << b
        kept = total.astype(bf16)
        other = swap(kept, "fsdp", half >> b)
        if meanwhile is not None:
            other = after(other, *meanwhile(kept))
        order = [i ^ step for i in range(half)]
        total = kept.astype(f32) + jnp.stack([other[i] for i in order]).astype(f32)
    return total


def to_owner(partial):
    held = partial
    mask = 1
    while held.shape[0] > 1:
        half = held.shape[0] // 2
        held = held[:half] + swap(held[half:].astype(bf16), "fsdp", mask).astype(f32)
        mask *= 2
    return held[0]


def reversed_bits(value, count):
    result = value * 0
    for b in range(bits_of(count)):
        result = result + ((value >> b) & 1) * (count >> (b + 1))
    return result


def on_device(
    inputs,
    block_order,
    cotangent,
    first_gain,
    first_shift,
    qkv_weight,
    qv_bias,
    proj_weight,
    proj_bias,
    second_gain,
    second_shift,
    fc_weight,
    fc_bias,
    down_weight,
    down_bias,
):
    nctx = lax.axis_size("ctx")
    nf = lax.axis_size("fsdp")
    c = lax.axis_index("ctx")
    f = lax.axis_index("fsdp")
    _, rows_dev, width = inputs.shape
    piece = width // nf
    heads = piece // HD
    ff = down_weight.shape[0]
    block_rows = rows_dev * nctx // block_order.shape[0]
    group = nctx // nf
    s, g = c // group, c % group
    half = nf // 2

    at = jnp.stack([f, s]).astype(jnp.int32)
    me = at[:1]
    own = inputs[0]
    tokens_b = [own]
    mask = nf // 2
    while mask:
        tokens_b = tokens_b + [swap(block, "fsdp", mask) for block in tokens_b]
        mask //= 2
    cut = kernel_call(cut_qkv_kernel, [((piece, 3 * piece), bf16)] * nf, (me,), (qkv_weight,))
    w_pieces = [swap(cut[k], "fsdp", k) if k else cut[k] for k in range(nf)]
    parts = [first_gain, first_shift, proj_bias, second_gain, second_shift, down_bias, qv_bias]
    parts = lax.optimization_barrier((*parts, tokens_b[1]))[:-1]
    vectors_all = [jnp.concatenate(parts).reshape(8, piece)]
    mask = nf // 2
    while mask:
        vectors_all = vectors_all + [swap(block, "fsdp", mask) for block in vectors_all]
        mask //= 2
    cut_fc = kernel_call(cut_fc_kernel, [((piece, ff), bf16)] * nf, (me,), (fc_weight,))

    shape_q, shape_kv = ((piece, rows_dev), bf16), ((2 * piece, rows_dev), bf16)
    results = kernel_call(
        functools.partial(project_kernel, nf),
        [shape_q] * nf
        + [shape_kv] * nf
        + [
            ((nf, rows_dev, width), bf16),
            ((nf, rows_dev, width), f32),
            ((nf, rows_dev, 128), f32),
            ((width, 3 * piece), bf16),
            ((8, width), f32),
        ],
        (at,),
        [after(w_pieces[0], cut_fc[0]), *tokens_b, *vectors_all, *w_pieces[1:]],
        scratch=[
            pltpu.VMEM((nf, rows_dev, width), bf16),
            pltpu.VMEM((nf, 8, piece), f32),
            pltpu.VMEM((nf, 3 * piece, rows_dev), bf16),
        ],
        cost=2 * nf * rows_dev * width * 3 * piece,
    )
    q_blocks, kv_blocks = results[:nf], results[nf : 2 * nf]
    hidden1, normed1, inverse1, w_qkv, flat = results[2 * nf :]
    pbias, gain2, shift2, dbias = (flat[i : i + 1] for i in range(2, 6))
    gain1 = flat[:1]
    tokens_half = jnp.stack(tokens_b[: nf // 2])

    def across(blocks):
        return [swap(b, "ctx", j * group) if j else b for j, b in enumerate(blocks)]

    kv_all = across(kv_blocks)
    q_blocks = across(q_blocks)
    upstream = [after(cotangent[0], kv_all[1])]
    mask = half
    while mask:
        upstream = upstream + [swap(block, "fsdp", mask) for block in upstream]
        mask //= 2
    fc_pieces = [
        swap(after(cut_fc[k], kv_all[1]), "fsdp", k) if k else cut_fc[k] for k in range(nf)
    ]
    mask = group // 2
    while mask:
        kv_all = kv_all + [swap(block, "ctx", mask) for block in kv_all]
        mask //= 2
    members = reversed_bits(jnp.arange(group, dtype=jnp.int32), group) ^ g
    own_group = s ^ jnp.arange(nf, dtype=jnp.int32)
    q_pos = positions_of(block_order, own_group * group + g, rows_dev, block_rows).reshape(1, -1)
    k_from = (own_group[None, :] * group + members[:, None]).reshape(-1)
    per_dev = rows_dev // block_rows
    stored = (k_from[:, None] * per_dev + jnp.arange(per_dev, dtype=jnp.int32)).reshape(-1)
    matches = stored[:, None] == jnp.arange(block_order.shape[0], dtype=jnp.int32)
    k_blocks = jnp.sum(jnp.where(matches, block_order, 0), axis=1)
    nq, nk = nf * rows_dev, nctx * rows_dev
    flops = 2 * heads * HD * nq * nk
    results = kernel_call(
        functools.partial(attend_kernel, nf, nctx, block_rows, heads),
        [((heads, nk, nq), bf16)] + [shape_q] * nf,
        (k_blocks,),
        [q_pos, *q_blocks, *kv_all],
        scratch=[pltpu.VMEM((nk, nq), f32)],
        cost=2 * flops,
        grid=(heads,),
        blocks={1 + nf + nctx: pl.BlockSpec((1, nk, nq), lambda h: (h, 0, 0))},
    )
    weights, att_out = results[0], results[1:]

    def collect(blocks, *points):
        out = jnp.zeros((nf,) + blocks[0].shape, blocks[0].dtype)
        for j, block in enumerate(across(blocks)):
            if points:
                block = after(block, *points)
            out = lax.dynamic_update_index_in_dim(out, block, s ^ j, 0)
        return out

    att = collect(att_out)

    part = dotf("pft,fo->pto", after(att, *fc_pieces, *upstream), proj_weight)
    total = sum_over_fsdp(part[:half], part[half:].astype(bf16))
    residual = tokens_half.astype(f32) + total + pbias
    normed2, inverse2 = normalize(residual)
    hidden2_half = (normed2 * gain2 + shift2).astype(bf16)
    rows_all = nf * rows_dev
    hidden2_half = hidden2_half.reshape(rows_all // 2, width)
    flops = 6 * rows_all * width * ff
    hidden2, up_rows, activation_b, pre_grad_b, second_keep, second_send, fc_sum = kernel_call(
        functools.partial(feed_kernel, nf),
        [
            ((rows_all, width), bf16),
            ((rows_all, width), bf16),
            ((rows_all, ff), bf16),
            ((rows_all, ff), bf16),
            ((rows_all // 2, width), f32),
            ((rows_all // 2, width), bf16),
            ((1, ff), f32),
        ],
        (me,),
        [hidden2_half, swap(hidden2_half, "fsdp", 1), *upstream, *fc_pieces]
        + [down_weight, fc_bias.reshape(1, ff)],
        scratch=[pltpu.VMEM((width, ff), bf16)],
        cost=flops,
    )

    nbits, gbits, sbits = bits_of(nctx), bits_of(group), bits_of(nf)
    bit = [(c >> b) & 1 for b in range(nbits)]
    state = {}

    def columns(value):
        w = value.shape[1] // 2
        return value[:, :w], value[:, w:]

    def step(name, halves, b):
        keep, send = begin(halves, bit[b])
        state[name] = (keep, send, swap(send, "ctx", 1 << b))
        return send

    def result_of(name, point=None):
        keep, _, came = state[name]
        if point is not None:
            came = after(came, point)
        return keep + came.astype(f32)

    down_order = [gbits] + [b for b in range(nbits) if b != gbits]

    def down_halves(value, b):
        left = down_order[down_order.index(b) :]
        axis = sum(1 for other in left if other > b)
        return lax.index_in_dim(value, 0, axis, False), lax.index_in_dim(value, 1, axis, False)

    def start_gradients(point):
        held = dotf("te,th->eh", after(hidden2, point), pre_grad_b)
        for b in reversed(range(gbits)):
            sent_fc = step("fc", columns(held), b)
            if b:
                held = result_of("fc")
        held = dotf("to,th->oh", after(up_rows, point), activation_b)
        held = held.reshape((2,) * nbits + (width // nctx, ff))
        sent_down = step("down", down_halves(held, down_order[0]), down_order[0])
        return sent_fc, sent_down

    second_keep = second_keep.reshape(half, rows_dev, width)
    second_send = second_send.reshape(half, rows_dev, width)
    second_grad = sum_over_fsdp(second_keep, second_send, start_gradients)
    up_half = up_rows[: rows_all // 2].reshape(half, rows_dev, width).astype(f32)
    residual_grad = up_half + norm_backward(second_grad, normed2, inverse2, gain2)
    rgrad_half = residual_grad.astype(bf16)
    rgrad_far = swap(rgrad_half, "fsdp", 1)
    rgrad, *do_blocks = kernel_call(
        functools.partial(turn_back_kernel, nf),
        [((nf, rows_dev, width), bf16)] + [shape_q] * nf,
        (at[1:],),
        [rgrad_half, rgrad_far, proj_weight],
        scratch=[pltpu.VMEM((nf, piece, rows_dev), bf16)],
        cost=2 * nf * rows_dev * width * piece,
    )

    do_blocks = across(do_blocks)

    def lowest(value):
        at = (slice(None),) * (value.ndim - 3)
        return value[at + (0,)], value[at + (1,)]

    held = result_of("fc", do_blocks[1])
    held = held.reshape((2,) * sbits + (piece, held.shape[1]))
    sent_fc = step("fc", lowest(held), gbits)
    held = result_of("down", do_blocks[1])
    sent_down = step("down", down_halves(held, down_order[1]), down_order[1])
    do_blocks[0] = after(do_blocks[0], sent_fc, sent_down)
    results = kernel_call(
        functools.partial(attend_back_kernel, nf, nctx, heads),
        [shape_q] * nf + [(shape_kv[0], f32)] * nf + [shape_kv] * (nctx - nf),
        (),
        [weights, *q_blocks, *do_blocks, *att_out, *kv_all],
        cost=10 * heads * HD * nq * nk,
        grid=(heads,),
        blocks={0: pl.BlockSpec((1, nk, nq), lambda h: (h, 0, 0))},
    )
    dq_blocks, dkv = results[:nf], results[nf:]
    dq_blocks = list(lax.optimization_barrier(tuple(dq_blocks)))
    mask = 1
    while len(dkv) > nf:
        h = len(dkv) // 2
        came = [swap(block.astype(bf16), "ctx", mask) for block in dkv[h:]]
        dkv = [mine.astype(f32) + other.astype(f32) for mine, other in zip(dkv[:h], came)]
        mask *= 2
    dkv_sent = [block.astype(bf16) for block in dkv]
    dq_own = collect(dq_blocks, *dkv_sent)
    dkv_own = collect(dkv_sent)
    block_out = residual[0] + to_owner(
        dotf("th,ho->to", after(activation_b, *dkv_sent), down_weight).reshape(nf, rows_dev, width)
    ) + dbias
    g_proj = dotf("pft,pto->fo", att, after(rgrad, *dkv_sent))
    step("proj", columns(g_proj), nbits - 1)
    qkv_grad = jnp.concatenate([dq_own, dkv_own], axis=1)

    device = c * nf + f
    sent = step("qkv", columns(dotf("pft,pte->fe", qkv_grad, hidden1)), 0)
    ends = {}
    fc_b, down_b = gbits + 1, 2
    while fc_b < nbits or down_b < nbits:
        if fc_b < nbits:
            ends["fc"] = step("fc", lowest(result_of("fc", sent)), fc_b)
            fc_b += 1
        if down_b < nbits:
            b = down_order[down_b]
            ends["down"] = step("down", down_halves(result_of("down", sent), b), b)
            down_b += 1

    qkv_grad = after(qkv_grad, sent, *ends.values())
    first_part = dotf("pft,ef->pte", qkv_grad, w_qkv)
    first_grad = to_owner(first_part)
    input_grad = residual_grad[0] + norm_backward(
        first_grad, normed1[0], after(inverse1, first_grad)[0, :, :1], gain1
    )
    up_late, fc_sum = lax.optimization_barrier((up_rows, fc_sum, *dkv_sent))[:2]
    sums = [
        jnp.sum(up_late[: rows_all // 2].astype(f32), axis=0),
        jnp.sum(residual_grad, axis=(0, 1)),
        jnp.sum(second_grad * normed2, axis=(0, 1)),
        jnp.sum(second_grad, axis=(0, 1)),
        jnp.sum(first_part * normed1, axis=(0, 1)),
        jnp.sum(first_part, axis=(0, 1)),
        fc_sum.reshape(-1),
        jnp.sum(qkv_grad[:, :piece].astype(f32), axis=(0, 2)),
        jnp.sum(qkv_grad[:, 2 * piece :].astype(f32), axis=(0, 2)),
    ]
    sums = jnp.concatenate(sums).reshape(-1, 128)
    held_twice = jnp.arange(sums.shape[0])[:, None] < 4 * width // 128
    sums = jnp.where(held_twice & (f >= half), 0.0, sums)

    def next_sums(b, *points):
        came = swap(sums, "ctx", 1 << b)
        return sums + (after(came, *points) if points else came)


    held = result_of("qkv")
    for b in range(1, sbits):
        sent = step("qkv", columns(held), b)
        sums = next_sums(b - 1, sent)
        step("proj", columns(result_of("proj", sent)), nbits - 1 - b)
        held = result_of("qkv")
    held = held.reshape((2,) * (nbits - sbits) + (-1, piece))
    for b in range(sbits, nbits):
        sent = step("qkv", lowest(held), b)
        sums = next_sums(b - 1, sent)
        step("proj", columns(result_of("proj", sent)), nbits - 1 - b)
        held = result_of("qkv")
    g_proj = result_of("proj")
    g_down = result_of("down", sent).T
    last = result_of("fc", sent).astype(bf16)
    pairs = []
    for cc in range(nctx):
        for fi in range(nf):
            pairs.append((cc * nf + fi, (fi * group + cc % group) * nf + cc // group))
    g_fc = lax.ppermute(last, ("ctx", "fsdp"), pairs).astype(f32)
    unit = width // nctx
    units = held.astype(bf16).reshape(3, unit, piece)
    got = []
    for i in range(3):
        pairs = []
        for cc in range(nctx):
            r = sum(((cc >> b) & 1) * (nf >> (b + 1)) for b in range(sbits))
            for fi in range(nf):
                row = ((cc >> sbits) * 3 + (i - group * fi) % 3) * unit
                column = (row // piece) * width + fi * piece + row % piece
                assert (column // unit) % 3 == i
                pairs.append((cc * nf + fi, (column // (3 * unit)) * nf + r))
        which = (i + 3 * group * nf - group * f) % 3
        sent = lax.dynamic_index_in_dim(units, which, 0, keepdims=False)
        got.append(lax.ppermute(sent, ("ctx", "fsdp"), pairs))
    g_qkv_own = jnp.concatenate(got, axis=0).T.astype(f32)

    sums = next_sums(nbits - 1, units)
    shared = 6 * width // 128
    pieces = [sums]
    mask = nf // 2
    while mask:
        pieces = pieces + [swap(block, "fsdp", mask) for block in pieces]
        mask //= 2
    six = sum(block[:shared] for block in pieces).reshape(6, width)

    def slice_of(index, first, last):
        chosen = jnp.zeros((last - first, 128), f32)
        for k, block in enumerate(pieces):
            is_it = (index ^ f) == reversed_bits(k, nf)
            chosen = jnp.where(is_it, block[first:last], chosen)
        return chosen.reshape(-1)

    size = width // (nctx * nf)
    own = lax.dynamic_slice_in_dim(six, device * size, size, 1)
    start = device * 2 * size
    part, rest = start // width, start % width
    ends = shared + ff // 128
    qv_own = lax.dynamic_slice_in_dim(
        slice_of(rest // piece, ends, sums.shape[0]), part * piece + rest % piece, 2 * size, 0
    )
    fsize = ff // nctx
    start = device * fsize
    fc_own = lax.dynamic_slice_in_dim(slice_of(start // ff, shared, ends), start % ff, fsize, 0)
    return (
        block_out.astype(bf16)[None],
        input_grad[None],
        own[4],
        own[5],
        g_qkv_own,
        qv_own,
        g_proj,
        own[1],
        own[2],
        own[3],
        g_fc,
        fc_own,
        g_down,
        own[0],
    )


def solution(mesh):
    vector, matrix = P("fsdp"), P("fsdp", None)
    placed = (
        P("fsdp", "ctx", None),
        P(),
        P("fsdp", "ctx", None),
        vector,
        vector,
        matrix,
        vector,
        matrix,
        vector,
        vector,
        vector,
        matrix,
        vector,
        matrix,
        vector,
    )
    spread, block = P(("ctx", "fsdp")), P("fsdp", "ctx")

    return jax.shard_map(
        on_device,
        mesh=mesh,
        in_specs=placed,
        out_specs=(
            P("fsdp", "ctx", None),
            P("fsdp", "ctx", None),
            spread,
            spread,
            block,
            spread,
            block,
            spread,
            spread,
            spread,
            block,
            spread,
            block,
            spread,
        ),
        check_vma=False,
    )
```
